256 devices in a mesh: row: 32 (over x, y, core), col: 8 (over z).
Axes of the slice: x: 4, y: 4, z: 8, core: 2. Of those that a mesh axis runs over, the one named last changes fastest.
Arguments:
- test_kernel: float32 [65536, 4096], P('row', 'col'), may hold values from -6 to 6
- first_panel: float32 [65536, 512], P('row', 'col'), may hold values from -0.25 to 0.25
- second_panel: float32 [65536, 512], P('row', 'col'), may hold values from -0.25 to 0.25
- first_inverse: float32 [512, 512], replicated, may hold values from -0.15 to 1.5, as said below
- second_inverse: float32 [512, 512], replicated, may hold values from -0.15 to 1.5, as said below
Outputs:
- solution: float32 [65536, 4096], P('row', 'col')
The draws below stay inside these ranges and needn't reach their ends.
Inputs may be any that keep to these rules, and one draw needn't show every extreme that they name: `first_inverse`: lower triangular: zeros above the diagonal, diagonal entries positive. `second_inverse`: lower triangular: zeros above the diagonal, diagonal entries positive.
All inputs are finite; a program needn't handle non-finite values.
Results may differ from the reference program's by a relative error of at most 0.000075.
Values sent between devices are 32-bit elements; how exact they have to be, the bound alone decides.
A program may use at most 64 MiB of HBM per device.

```python
import jax
import jax.numpy as jnp
from jax import lax

B = 512
ROWS_DEV = 2048
ROWS = 65536
TESTS = 4096


def triangle_draw(key, which):
    base = jax.random.fold_in(key, which)
    key_diagonal = jax.random.fold_in(base, 1)
    key_lower = jax.random.fold_in(base, 2)
    diagonal_part = jax.random.uniform(key_diagonal, (B,), jnp.float32, 0.6, 1.4)
    lower_part = jnp.clip(0.03 * jax.random.normal(key_lower, (B, B), jnp.float32), -0.15, 0.15)
    row_index = jnp.arange(B)[:, None]
    column_index = jnp.arange(B)[None, :]
    strict_lower = jnp.where(row_index > column_index, lower_part, 0.0)
    return strict_lower + jnp.where(row_index == column_index, diagonal_part[:, None], 0.0)


def draw_first_inverse(key, part):
    return triangle_draw(key, 11)


def draw_second_inverse(key, part):
    return triangle_draw(key, 23)


def block_scale(key, extent, pieces, low, top_value):
    def one(dim, parts):
        heights = jax.random.uniform(jax.random.fold_in(jax.random.fold_in(key, 6), dim), (parts,), jnp.float32, low / len(pieces), top_value / len(pieces))
        return jnp.repeat(jnp.exp(heights), extent[dim] // parts).reshape((-1,) + (1,) * (len(extent) - dim - 1))

    gain = one(*pieces[0])
    for cut in pieces[1:]:
        gain = gain * one(*cut)
    return gain


def centred(own_key, dims, spread, reach, pieces=(), dtype=jnp.bfloat16):
    entries = jax.random.normal(own_key, dims, jnp.float32) * spread
    if len(pieces) > 0:
        entries = block_scale(own_key, dims, pieces, -0.22, 0.18) * entries
    return jnp.clip(entries, min=-reach, max=reach).astype(dtype)


def setup_inputs(seed: int = 0) -> dict:
    streams_of = jax.random.split(jax.random.key(seed), 6)
    test_kernel = centred(streams_of[0], (ROWS, TESTS), 1.0, 6.0, ((0, 32), (1, 8)), jnp.float32)
    first_panel = centred(streams_of[1], (ROWS, B), B ** -0.5, 0.25, ((0, 32), (1, 8)), jnp.float32)
    second_panel = centred(streams_of[2], (ROWS, B), B ** -0.5, 0.25, ((0, 32), (1, 8)), jnp.float32)
    first_inverse = draw_first_inverse(jax.random.fold_in(streams_of[5], 71), 0)
    second_inverse = draw_second_inverse(jax.random.fold_in(streams_of[5], 71), 0)
    return {"test_kernel": test_kernel, "first_panel": first_panel, "second_panel": second_panel, "first_inverse": first_inverse, "second_inverse": second_inverse}


def product(left, right):
    return jnp.dot(left, right, precision=lax.Precision.HIGHEST, preferred_element_type=jnp.float32)


def reference(test_kernel, first_panel, second_panel, first_inverse, second_inverse):
    first_solved = product(first_inverse, test_kernel[:B])
    partial_value = test_kernel - product(first_panel, first_solved)
    second_solved = product(second_inverse, partial_value[ROWS_DEV:ROWS_DEV + B])
    final = partial_value - product(second_panel, second_solved)
    final = final.at[:B].set(first_solved)
    final = final.at[ROWS_DEV:ROWS_DEV + B].set(second_solved)
    return final
```

```python
import jax
import jax.numpy as jnp
from jax import lax
from jax.experimental import pallas as pl
from jax.experimental.pallas import tpu as pltpu
from jax.sharding import PartitionSpec as P

MESH = pl.DeviceIdType.MESH
F32 = jnp.float32
BF16 = jnp.bfloat16
NX, NY = 4, 4
SIDES = (0, 1)


def split(value):
    high = value.astype(BF16)
    return high, (value - high.astype(F32)).astype(BF16)


def product(left, right_high, right_low):
    high, low = split(left)

    def dot(a, b):
        return jnp.dot(a, b, preferred_element_type=F32)

    return dot(high, right_high) + (dot(low, right_high) + dot(high, right_low))


def kernel(
    t_hbm, p1_hbm, p2_hbm, inv1, inv2, out_hbm,
    pg, pb, t1, t2, acc, s1, s2, sh, sl, rh, rl,
    zs, zr, xs, xr, local, tload, oload,
):
    nz = pg.shape[1]
    kc = pg.shape[2]
    half = nz // 2
    block = t1.shape[0]
    nblocks = acc.shape[0] // block
    npieces = 2 * nblocks
    xp = block // nz
    row = lax.axis_index("row")
    z = lax.axis_index("col")
    core = lax.rem(row, 2)
    y = lax.rem(row // 2, NY)
    x = row // (2 * NY)

    def at(xx, yy, cc):
        return (xx * NY + yy) * 2 + cc

    sibling = at(x, y, 1 - core)
    source = jnp.logical_and(x == 0, y == 0)
    other = jnp.logical_not(source)
    panels = (p1_hbm, p2_hbm)

    def origin(k):
        return lax.rem(z + (k + nz), nz)

    barrier = pltpu.get_barrier_semaphore()
    neighbours = (
        (row, origin(1)),
        (row, origin(-1)),
        (at(lax.rem(x + 1, NX), y, core), z),
        (at(lax.rem(x + NX - 1, NX), y, core), z),
        (at(x, lax.rem(y + 1, NY), core), z),
        (at(x, lax.rem(y + NY - 1, NY), core), z),
        (sibling, z),
    )

    def load_rows(b):
        part = pl.ds(b * block, block)
        return pltpu.make_async_copy(t_hbm.at[part], acc.at[part], tload.at[b])

    def own_panel(p):
        return pltpu.make_async_copy(panels[p], pg.at[p, z], local.at[p])

    for b in range(nblocks):
        load_rows(b).start()
    for p in range(2):
        own_panel(p).start()
    for n in neighbours:
        pl.semaphore_signal(barrier, inc=1, device_id=n, device_id_type=MESH)
    pl.semaphore_wait(barrier, len(neighbours))

    def where(j):
        return j // nblocks, pl.ds((j % nblocks) * block, block)

    def hops(side, j):
        return half if (j % 2 == side) else half - 1

    def zsend(side, h, j):
        if h > hops(side, j):
            return
        p, lanes = where(j)
        sign = -1 if side == 0 else 1
        owner = origin(sign * (h - 1))
        src = panels[p].at[:, lanes] if h == 1 else pg.at[p, owner, :, lanes]
        pltpu.make_async_remote_copy(
            src_ref=src,
            dst_ref=pg.at[p, owner, :, lanes],
            send_sem=zs.at[side, h - 1],
            recv_sem=zr.at[side, h - 1, j],
            device_id=(row, origin(-sign)),
            device_id_type=MESH,
        ).start()

    def zwait(side, h, j):
        if h > hops(side, j):
            return
        p, lanes = where(j)
        owner = origin(-h if side == 0 else h)
        ref = pg.at[p, owner, :, lanes]
        pltpu.make_async_remote_copy(
            src_ref=ref,
            dst_ref=ref,
            send_sem=zs.at[side, h - 1],
            recv_sem=zr.at[side, h - 1, j],
            device_id=(row, origin(1)),
            device_id_type=MESH,
        ).wait_recv()

    def first(j):
        for side in SIDES:
            zsend(side, 1, j)

    def forward(h, j):
        for side in SIDES:
            zwait(side, h, j)
            zsend(side, h + 1, j)

    buffers = (t1, t2, pb)
    order = [0]
    for d in range(1, half):
        order += [-d, d]
    order += [half]

    def piece(array, i):
        index = i if array < 2 else origin(order[i])
        return pl.ds(pl.multiple_of(index * xp, xp), xp)

    def xcopy(array, i, slot, src, target):
        return pltpu.make_async_remote_copy(
            src_ref=src,
            dst_ref=buffers[array].at[piece(array, i)],
            send_sem=xs.at[array, slot],
            recv_sem=xr.at[array, i],
            device_id=(target, z),
            device_id_type=MESH,
        )

    def to_children(array, i, src):
        @pl.when(jnp.logical_and(y == 0, x <= 1))
        def _():
            xcopy(array, i, 0, src, at(x + 1, y, core)).start()

        @pl.when(jnp.logical_and(y == 0, x == 0))
        def _():
            xcopy(array, i, 1, src, at(NX - 1, y, core)).start()

        @pl.when(y <= 1)
        def _():
            xcopy(array, i, 2, src, at(x, y + 1, core)).start()

        @pl.when(y == 0)
        def _():
            xcopy(array, i, 3, src, at(x, NY - 1, core)).start()

        xcopy(array, i, 4, src, sibling).start()

    def xwait(array, i):
        ref = buffers[array].at[piece(array, i)]
        xcopy(array, i, 4, ref, sibling).wait_recv()

    def xforward(array, i):
        xwait(array, i)

        @pl.when(core == min(array, 1))
        def _():
            to_children(array, i, buffers[array].at[piece(array, i)])

    def drain(array):
        whole = buffers[array]

        def wait(slot):
            pltpu.make_async_remote_copy(
                src_ref=whole, dst_ref=whole, send_sem=xs.at[array, slot], recv_sem=xr.at[array, 0],
                device_id=(sibling, z), device_id_type=MESH,
            ).wait_send()

        @pl.when(core == min(array, 1))
        def _():
            @pl.when(jnp.logical_and(y == 0, x <= 1))
            def _():
                wait(0)

            @pl.when(jnp.logical_and(y == 0, x == 0))
            def _():
                wait(1)

            @pl.when(y <= 1)
            def _():
                wait(2)

            @pl.when(y == 0)
            def _():
                wait(3)

            wait(4)

    def keep_rows(array):
        return pltpu.make_async_copy(t_hbm.at[pl.ds(0, block)], buffers[array], local.at[2])

    def keep_panel(i):
        return pltpu.make_async_copy(
            pg.at[0, origin(order[i]), :, pl.ds(0, block)], pb.at[piece(2, i)], local.at[3]
        )

    def panel_piece(i):
        src = pg.at[0, origin(order[i]), :, pl.ds(0, block)]

        @pl.when(core == 1)
        def _():
            to_children(2, i, src)
            keep_panel(i).start()

    @pl.when(source)
    def _():
        for array in range(2):
            @pl.when(core == array)
            def _():
                keep_rows(array).start()
                for i in range(nz):
                    to_children(array, i, t_hbm.at[pl.ds(i * xp, xp)])

        first(0)
        first(1)
        own_panel(0).wait()
        panel_piece(0)
        for h in range(1, half):
            forward(h, 0)
            first(h + 1)
            panel_piece(2 * h - 1)
            panel_piece(2 * h)
        for j in range(half + 1, npieces):
            first(j)
        zwait(0, half, 0)
        panel_piece(nz - 1)
        for array in range(2):
            @pl.when(core == array)
            def _():
                keep_rows(array).wait()

            @pl.when(core != array)
            def _():
                for i in range(nz):
                    xwait(array, i)
        for j in range(1, npieces):
            forward(1, j)

    @pl.when(other)
    def _():
        for j in range(npieces):
            first(j)
        own_panel(0).wait()
        for i in range(nz):
            xforward(0, i)
            xforward(1, i)
            if i < npieces:
                forward(1, i)

    own_panel(1).wait()

    tile = 256

    def solve(inverse, into):
        @pl.loop(0, block // tile)
        def _(i):
            rows = pl.ds(pl.multiple_of(i * tile, tile), tile)
            into[rows, :] = product(inverse[rows, :], rh[...], rl[...])

    def keep_split(p, value):
        high, low = split(value)
        sh[p] = high
        sl[p] = low

    rh[...], rl[...] = split(t1[...])
    solve(inv1, s1)
    keep_split(0, s1[...])

    @pl.when(source)
    def _():
        for j in range(1, npieces):
            forward(2, j)

        @pl.when(core == 1)
        def _():
            whole = pltpu.make_async_copy(pb, pb, local.at[3])
            whole.wait()

        @pl.when(core == 0)
        def _():
            for i in range(nz):
                xwait(2, i)

    @pl.when(other)
    def _():
        for i in range(nz):
            xforward(2, i)
            if i < npieces:
                forward(2, i)

    @pl.loop(0, block // tile)
    def _(i):
        lanes = pl.ds(pl.multiple_of(i * tile, tile), tile)
        value = t2[lanes, :] - product(pb[:, lanes].T, sh[0], sl[0])
        rh[lanes, :], rl[lanes, :] = split(value)

    solve(inv2, s2)
    keep_split(1, s2[...])

    for b in range(nblocks):
        load_rows(b).wait()

    def update(b, origins):
        ks = [pl.ds(pl.multiple_of(o * kc, kc), kc) for o in origins]
        right_high = jnp.concatenate([sh[p, k, :] for k in ks for p in range(2)], axis=0)
        right_low = jnp.concatenate([sl[p, k, :] for k in ks for p in range(2)], axis=0)

        @pl.loop(0, block // tile)
        def _(i):
            rows = pl.ds(pl.multiple_of(b * block + i * tile, tile), tile)
            left = jnp.concatenate([pg[p, o, :, rows] for o in origins for p in range(2)], axis=0)
            acc[rows, :] = acc[rows, :] - product(left.T, right_high, right_low)

    units = [(b, d) for d in (1, 2) for b in range(nblocks)]
    for j in range(npieces):
        if j == 0:
            @pl.when(other)
            def _():
                forward(half - 1, 0)
        else:
            forward(half - 1, j)
        if j < len(units):
            b, d = units[j]
            update(b, (origin(-d), origin(d)))
    for b in range(nblocks):
        update(b, (origin(-3), origin(3)))
    for b in range(nblocks):
        update(b, (z,))

    def store_rows(b):
        part = pl.ds(b * block, block)
        return pltpu.make_async_copy(acc.at[part], out_hbm.at[part], oload.at[b])

    for b in range(nblocks):
        for j in (b, b + nblocks):
            for side in SIDES:
                if j == 0:
                    @pl.when(other)
                    def _():
                        zwait(side, half, 0)
                else:
                    zwait(side, half, j)
        update(b, (origin(half),))
        if b == 0:
            @pl.when(row == 0)
            def _():
                acc[pl.ds(0, block), :] = s1[...]

            @pl.when(row == 1)
            def _():
                acc[pl.ds(0, block), :] = s2[...]
        store_rows(b).start()

    for side in SIDES:
        for h in range(1, half + 1):
            ref = pg.at[:, z] if h < half else pg.at[0, z]
            pltpu.make_async_remote_copy(
                src_ref=ref, dst_ref=ref, send_sem=zs.at[side, h - 1], recv_sem=zr.at[side, h - 1, 0],
                device_id=(row, origin(1)), device_id_type=MESH,
            ).wait_send()
    for array in range(3):
        drain(array)
    for b in range(nblocks):
        store_rows(b).wait()


def per_device(nz, test_kernel, first_panel, second_panel, first_inverse, second_inverse):
    rows, cols = test_kernel.shape
    kc = first_panel.shape[1]
    block = first_inverse.shape[0]
    vmem = pl.BlockSpec(memory_space=pltpu.VMEM)
    hbm = pl.BlockSpec(memory_space=pl.ANY)
    dma = pltpu.SemaphoreType.DMA
    nblocks = rows // block
    return pl.pallas_call(
        kernel,
        out_shape=jax.ShapeDtypeStruct((rows, cols), F32),
        in_specs=[hbm, hbm, hbm, vmem, vmem],
        out_specs=hbm,
        scratch_shapes=[
            pltpu.VMEM((2, nz, kc, rows), F32),
            pltpu.VMEM((block, block), F32),
            pltpu.VMEM((block, cols), F32),
            pltpu.VMEM((block, cols), F32),
            pltpu.VMEM((rows, cols), F32),
            pltpu.VMEM((block, cols), F32),
            pltpu.VMEM((block, cols), F32),
            pltpu.VMEM((2, block, cols), BF16),
            pltpu.VMEM((2, block, cols), BF16),
            pltpu.VMEM((block, cols), BF16),
            pltpu.VMEM((block, cols), BF16),
            dma((2, nz // 2)),
            dma((2, nz // 2, 2 * nblocks)),
            dma((3, 5)),
            dma((3, nz)),
            dma((4,)),
            dma((nblocks,)),
            dma((nblocks,)),
        ],
        compiler_params=pltpu.CompilerParams(
            collective_id=0, has_side_effects=True, vmem_limit_bytes=40 * 1024 * 1024
        ),
    )(test_kernel, first_panel.T, second_panel.T, first_inverse, second_inverse)


def solution(mesh):
    nz = mesh.shape["col"]

    def run(*args):
        return per_device(nz, *args)

    in_specs = (P("row", "col"), P("row", "col"), P("row", "col"), P(), P())
    return jax.shard_map(run, mesh=mesh, in_specs=in_specs, out_specs=P("row", "col"), check_vma=False)
```

```python
import functools

import jax
import jax.numpy as jnp
from jax import lax
from jax.experimental import pallas as pl
from jax.experimental.pallas import tpu as pltpu
from jax.sharding import PartitionSpec as P

MESH = pl.DeviceIdType.MESH
F32 = jnp.float32
BF16 = jnp.bfloat16
NX, NY = 4, 4
SIDES = (0, 1)
VMEM_BYTES = 60 * 1024 * 1024
CHUNKS = 4


def split(value):
    high = value.astype(BF16)
    return high, (value - high.astype(F32)).astype(BF16)


def dot(left, right):
    return jnp.dot(left, right, preferred_element_type=F32)


def product(left, right_high, right_low):
    high, low = split(left)
    return dot(high, right_high) + (dot(low, right_high) + dot(high, right_low))


def turned_product(left, right_high, right_low):
    high, low = split(left)
    high, low = high.T, low.T
    return dot(
        jnp.concatenate([high, low, high], axis=1),
        jnp.concatenate([right_high, right_high, right_low], axis=0),
    )


def kernel(
    t_hbm, p1_hbm, p2_hbm, inv1, inv2, acc_hbm, last_hbm, right_hbm,
    pg, pb, t1, t2, acc, s1, s2, sh, sl, rh, rl, right,
    zs, zr, xs, xr, local, tload, oload,
):
    nz = pg.shape[1]
    kc = pg.shape[2]
    half = nz // 2
    block = t1.shape[0]
    nblocks = acc.shape[0] // block
    npieces = 2 * nblocks
    xp = block // nz
    row = lax.axis_index("row")
    z = lax.axis_index("col")
    core = lax.rem(row, 2)
    y = lax.rem(row // 2, NY)
    x = row // (2 * NY)

    def at(xx, yy, cc):
        return (xx * NY + yy) * 2 + cc

    sibling = at(x, y, 1 - core)
    source = jnp.logical_and(x == 0, y == 0)
    other = jnp.logical_not(source)
    panels = (p1_hbm, p2_hbm)

    def origin(k):
        return lax.rem(z + (k + nz), nz)

    barrier = pltpu.get_barrier_semaphore()
    neighbours = (
        (row, origin(1)),
        (row, origin(-1)),
        (at(lax.rem(x + 1, NX), y, core), z),
        (at(lax.rem(x + NX - 1, NX), y, core), z),
        (at(x, lax.rem(y + 1, NY), core), z),
        (at(x, lax.rem(y + NY - 1, NY), core), z),
        (sibling, z),
    )

    def load_rows(b):
        part = pl.ds(b * block, block)
        return pltpu.make_async_copy(t_hbm.at[part], acc.at[part], tload.at[b])

    def own_panel(p):
        return pltpu.make_async_copy(panels[p], pg.at[p, z], local.at[p])

    for b in range(nblocks):
        load_rows(b).start()
    for p in range(2):
        own_panel(p).start()
    for n in neighbours:
        pl.semaphore_signal(barrier, inc=1, device_id=n, device_id_type=MESH)
    pl.semaphore_wait(barrier, len(neighbours))

    def where(j):
        return j // nblocks, pl.ds((j % nblocks) * block, block)

    def hops(side, j):
        return half if (j % 2 == side) else half - 1

    def zsend(side, h, j):
        if h > hops(side, j):
            return
        p, lanes = where(j)
        sign = -1 if side == 0 else 1
        owner = origin(sign * (h - 1))
        src = panels[p].at[:, lanes] if h == 1 else pg.at[p, owner, :, lanes]
        dst = last_hbm.at[p, :, lanes] if h == half else pg.at[p, owner, :, lanes]
        pltpu.make_async_remote_copy(
            src_ref=src,
            dst_ref=dst,
            send_sem=zs.at[side, h - 1],
            recv_sem=zr.at[side, h - 1, j],
            device_id=(row, origin(-sign)),
            device_id_type=MESH,
        ).start()

    def zwait(side, h, j):
        if h > hops(side, j):
            return
        p, lanes = where(j)
        owner = origin(-h if side == 0 else h)
        ref = last_hbm.at[p, :, lanes] if h == half else pg.at[p, owner, :, lanes]
        pltpu.make_async_remote_copy(
            src_ref=ref,
            dst_ref=ref,
            send_sem=zs.at[side, h - 1],
            recv_sem=zr.at[side, h - 1, j],
            device_id=(row, origin(1)),
            device_id_type=MESH,
        ).wait_recv()

    def first(j):
        for side in SIDES:
            zsend(side, 1, j)

    def forward(h, j):
        for side in SIDES:
            zwait(side, h, j)
            zsend(side, h + 1, j)

    buffers = (t1, t2, pb)
    order = [0]
    for d in range(1, half):
        order += [-d, d]
    order += [half]

    def piece(array, i):
        index = i if array < 2 else origin(order[i])
        return pl.ds(pl.multiple_of(index * xp, xp), xp)

    def xcopy(array, i, slot, src, target):
        return pltpu.make_async_remote_copy(
            src_ref=src,
            dst_ref=buffers[array].at[piece(array, i)],
            send_sem=xs.at[array, i % 2, slot],
            recv_sem=xr.at[array, i],
            device_id=(target, z),
            device_id_type=MESH,
        )

    def edges(tree):
        u, v = x, y

        def to(uu, vv):
            return at(uu, vv, core)

        return (
            (jnp.logical_and(v == 0, u <= 1), to(lax.rem(u + 1, NX), v)),
            (jnp.logical_and(v == 0, u == 0), to(NX - 1, v)),
            (v <= 1, to(u, lax.rem(v + 1, NX))),
            (v == 0, to(u, NX - 1)),
        )

    def to_children(array, i, src):
        for slot, (sends, target) in enumerate(edges(i % 2)):
            @pl.when(sends)
            def _():
                xcopy(array, i, slot, src, target).start()

        xcopy(array, i, 4, src, sibling).start()

    def xwait(array, i):
        ref = buffers[array].at[piece(array, i)]
        xcopy(array, i, 4, ref, sibling).wait_recv()

    def xforward(array, i):
        xwait(array, i)

        @pl.when(core == min(array, 1))
        def _():
            to_children(array, i, buffers[array].at[piece(array, i)])

    def drain(array):
        pieces = buffers[array].at[pl.ds(0, block // 2)]

        def wait(tree, slot):
            pltpu.make_async_remote_copy(
                src_ref=pieces, dst_ref=pieces, send_sem=xs.at[array, tree, slot], recv_sem=xr.at[array, 0],
                device_id=(sibling, z), device_id_type=MESH,
            ).wait_send()

        @pl.when(core == min(array, 1))
        def _():
            for tree in range(2):
                for slot, (sends, _unused) in enumerate(edges(tree)):
                    @pl.when(sends)
                    def _():
                        wait(tree, slot)

                wait(tree, 4)

    def keep_rows(array):
        return pltpu.make_async_copy(t_hbm.at[pl.ds(0, block)], buffers[array], local.at[2])

    def held_piece(i):
        lanes = pl.ds(0, block)
        if order[i] == half:
            return last_hbm.at[0, :, lanes]
        return pg.at[0, origin(order[i]), :, lanes]

    def keep_panel(i):
        return pltpu.make_async_copy(held_piece(i), pb.at[piece(2, i)], local.at[3])

    def panel_piece(i):
        src = held_piece(i)

        @pl.when(core == 1)
        def _():
            to_children(2, i, src)
            keep_panel(i).start()

    @pl.when(source)
    def _():
        for array in range(2):
            @pl.when(core == array)
            def _():
                keep_rows(array).start()
                for i in range(nz):
                    to_children(array, i, t_hbm.at[pl.ds(i * xp, xp)])

        first(0)
        first(1)
        own_panel(0).wait()
        panel_piece(0)
        for h in range(1, half):
            forward(h, 0)
            first(h + 1)
            panel_piece(2 * h - 1)
            panel_piece(2 * h)
        for j in range(half + 1, npieces):
            first(j)
        zwait(0, half, 0)
        panel_piece(nz - 1)
        for array in range(2):
            @pl.when(core == array)
            def _():
                keep_rows(array).wait()

            @pl.when(core != array)
            def _():
                for i in range(nz):
                    xwait(array, i)
        for j in range(1, npieces):
            forward(1, j)

    @pl.when(other)
    def _():
        for j in range(npieces):
            first(j)
        own_panel(0).wait()
        for i in range(nz):
            xforward(0, i)
            xforward(1, i)
            if i < npieces:
                forward(1, i)

    own_panel(1).wait()

    def keep_split(p, value):
        high, low = split(value)
        sh[p] = high
        sl[p] = low

    rh[...], rl[...] = split(t1[...])
    s1[...] = product(inv1[...], rh[...], rl[...])
    keep_split(0, s1[...])

    @pl.when(source)
    def _():
        for j in range(1, nblocks):
            forward(2, j)

        @pl.when(core == 1)
        def _():
            pltpu.make_async_copy(pb, pb, local.at[3]).wait()

        @pl.when(core == 0)
        def _():
            for i in range(nz):
                xwait(2, i)

    @pl.when(other)
    def _():
        for i in range(nz):
            xforward(2, i)
            if i >= half:
                forward(2, i - half)

    rh[...], rl[...] = split(t2[...] - turned_product(pb[...], sh[0], sl[0]))
    s2[...] = product(inv2[...], rh[...], rl[...])
    keep_split(1, s2[...])

    def update(b, origins):
        ks = [pl.ds(pl.multiple_of(o * kc, kc), kc) for o in origins]
        rows = pl.ds(b * block, block)
        acc[rows, :] = acc[rows, :] - turned_product(
            jnp.concatenate([pg[p, o, :, rows] for o in origins for p in range(2)], axis=0),
            jnp.concatenate([sh[p, k, :] for k in ks for p in range(2)], axis=0),
            jnp.concatenate([sl[p, k, :] for k in ks for p in range(2)], axis=0),
        )

    near = (z, origin(-1), origin(1))
    far = (origin(-2), origin(2), origin(-3), origin(3))
    for b in range(nblocks):
        forward(2, nblocks + b)
        load_rows(b).wait()
        update(b, near)

    def store_rows(b):
        part = pl.ds(b * block, block)
        return pltpu.make_async_copy(acc.at[part], acc_hbm.at[part], oload.at[b])

    for j in range(npieces):
        if j == 0:
            @pl.when(other)
            def _():
                forward(half - 1, 0)
        else:
            forward(half - 1, j)
        if j >= nblocks:
            b = j - nblocks
            update(b, far)
            if b == 0:
                @pl.when(row == 0)
                def _():
                    acc[pl.ds(0, block), :] = s1[...]

                @pl.when(row == 1)
                def _():
                    acc[pl.ds(0, block), :] = s2[...]
            store_rows(b).start()

    final = pl.ds(pl.multiple_of(origin(half) * kc, kc), kc)
    for p in range(2):
        right[0, pl.ds(p * kc, kc), :] = sh[p, final, :]
        right[1, pl.ds(p * kc, kc), :] = sl[p, final, :]
    store_right = pltpu.make_async_copy(right, right_hbm, local.at[2])
    store_right.start()
    for j in range(npieces):
        for side in SIDES:
            if j == 0:
                @pl.when(other)
                def _():
                    zwait(side, half, 0)
            else:
                zwait(side, half, j)

    for side in SIDES:
        for h in range(1, half + 1):
            ref = pg.at[:, z] if h < half else pg.at[0, z]
            pltpu.make_async_remote_copy(
                src_ref=ref, dst_ref=ref, send_sem=zs.at[side, h - 1], recv_sem=zr.at[side, h - 1, 0],
                device_id=(row, origin(1)), device_id_type=MESH,
            ).wait_send()
    for array in range(3):
        drain(array)
    store_right.wait()
    for b in range(nblocks):
        store_rows(b).wait()


def finish(block, acc_hbm, last_hbm, right_hbm, out_hbm, acc, last, right, sems):
    tile = acc.shape[0] // CHUNKS
    first_block = jnp.logical_not(lax.axis_index("row") < 2)
    loads, stores = [], []
    load_right = pltpu.make_async_copy(right_hbm, right, sems.at[3, 0])
    load_right.start()
    for i in range(CHUNKS):
        part = pl.ds(i * tile, tile)
        loads.append(
            (
                pltpu.make_async_copy(last_hbm.at[:, :, part], last.at[:, :, part], sems.at[0, i]),
                pltpu.make_async_copy(acc_hbm.at[part], acc.at[part], sems.at[1, i]),
            )
        )
        stores.append(pltpu.make_async_copy(acc.at[part], out_hbm.at[part], sems.at[2, i]))
        for copy in loads[-1]:
            copy.start()
    load_right.wait()
    for i in range(CHUNKS):
        part = pl.ds(i * tile, tile)
        for copy in loads[i]:
            copy.wait()

        def change():
            left = jnp.concatenate([last[p, :, part] for p in range(2)], axis=0)
            acc[part, :] = acc[part, :] - turned_product(left, right[0], right[1])

        if i * tile < block:
            pl.when(first_block)(change)
        else:
            change()
        stores[i].start()
    for copy in stores:
        copy.wait()


def per_device(nz, test_kernel, first_panel, second_panel, first_inverse, second_inverse):
    rows, cols = test_kernel.shape
    kc = first_panel.shape[1]
    block = first_inverse.shape[0]
    vmem = pl.BlockSpec(memory_space=pltpu.VMEM)
    hbm = pl.BlockSpec(memory_space=pl.ANY)
    dma = pltpu.SemaphoreType.DMA
    nblocks = rows // block
    acc, last, right = pl.pallas_call(
        kernel,
        out_shape=[
            jax.ShapeDtypeStruct((rows, cols), F32),
            jax.ShapeDtypeStruct((2, kc, rows), F32),
            jax.ShapeDtypeStruct((2, 2 * kc, cols), BF16),
        ],
        in_specs=[hbm, hbm, hbm, vmem, vmem],
        out_specs=[hbm, hbm, hbm],
        scratch_shapes=[
            pltpu.VMEM((2, nz, kc, rows), F32),
            pltpu.VMEM((block, block), F32),
            pltpu.VMEM((block, cols), F32),
            pltpu.VMEM((block, cols), F32),
            pltpu.VMEM((rows, cols), F32),
            pltpu.VMEM((block, cols), F32),
            pltpu.VMEM((block, cols), F32),
            pltpu.VMEM((2, block, cols), BF16),
            pltpu.VMEM((2, block, cols), BF16),
            pltpu.VMEM((block, cols), BF16),
            pltpu.VMEM((block, cols), BF16),
            pltpu.VMEM((2, 2 * kc, cols), BF16),
            dma((2, nz // 2)),
            dma((2, nz // 2, 2 * nblocks)),
            dma((3, 2, 5)),
            dma((3, nz)),
            dma((4,)),
            dma((nblocks,)),
            dma((nblocks,)),
        ],
        compiler_params=pltpu.CompilerParams(
            collective_id=0, has_side_effects=True, vmem_limit_bytes=VMEM_BYTES
        ),
    )(test_kernel, first_panel.T, second_panel.T, first_inverse, second_inverse)
    return pl.pallas_call(
        functools.partial(finish, block),
        out_shape=jax.ShapeDtypeStruct((rows, cols), F32),
        in_specs=[hbm, hbm, hbm],
        out_specs=hbm,
        scratch_shapes=[
            pltpu.VMEM((rows, cols), F32),
            pltpu.VMEM((2, kc, rows), F32),
            pltpu.VMEM((2, 2 * kc, cols), BF16),
            dma((4, CHUNKS)),
        ],
        compiler_params=pltpu.CompilerParams(vmem_limit_bytes=VMEM_BYTES),
    )(acc, last, right)


def solution(mesh):
    nz = mesh.shape["col"]

    def run(*args):
        return per_device(nz, *args)

    in_specs = (P("row", "col"), P("row", "col"), P("row", "col"), P(), P())
    return jax.shard_map(run, mesh=mesh, in_specs=in_specs, out_specs=P("row", "col"), check_vma=False)
```

```python
import functools

import jax
import jax.numpy as jnp
from jax import lax
from jax.experimental import pallas as pl
from jax.experimental.pallas import tpu as pltpu
from jax.sharding import PartitionSpec as P

MESH = pl.DeviceIdType.MESH
F32 = jnp.float32
BF16 = jnp.bfloat16
NX, NY = 4, 4
SIDES = (0, 1)
VMEM_BYTES = 36 * 1024 * 1024
FINISH_BYTES = 12 * 1024 * 1024
EARLY = 2
CHUNKS = 4


def split(value):
    high = value.astype(BF16)
    return high, (value - high.astype(F32)).astype(BF16)


def dot(left, right):
    return jnp.dot(left, right, preferred_element_type=F32)


def product(left, right_high, right_low):
    high, low = split(left)
    return dot(high, right_high) + (dot(low, right_high) + dot(high, right_low))


def turned_product(left, right_high, right_low):
    high, low = split(left)
    high, low = high.T, low.T
    return dot(
        jnp.concatenate([high, low, high], axis=1),
        jnp.concatenate([right_high, right_high, right_low], axis=0),
    )


def finish_block(part, first, out, acc, last, right):

    def change():
        left = jnp.concatenate([last[p, :, part] for p in range(2)], axis=0)
        out[part, :] = acc[part, :] - turned_product(left, right[0], right[1])

    if first:
        pl.when(lax.axis_index("row") >= 2)(change)
    else:
        change()


def kernel(
    t_hbm, p1_hbm, p2_hbm, inv1_hbm, inv2_hbm, acc, last, right,
    pg, pb, t1, t2, inv1, inv2, s1, s2, sh, sl, rh, rl,
    zs, zr, xs, xr, local, tload,
):
    nz = pg.shape[1]
    kc = pg.shape[2]
    half = nz // 2
    block = t1.shape[0]
    nblocks = acc.shape[0] // block
    npieces = 2 * nblocks
    xp = block // nz
    row = lax.axis_index("row")
    z = lax.axis_index("col")
    core = lax.rem(row, 2)
    y = lax.rem(row // 2, NY)
    x = row // (2 * NY)

    def at(xx, yy, cc):
        return (xx * NY + yy) * 2 + cc

    sibling = at(x, y, 1 - core)
    source = jnp.logical_and(x == 0, y == 0)
    other = jnp.logical_not(source)
    panels = (p1_hbm, p2_hbm)

    def origin(k):
        return lax.rem(z + (k + nz), nz)

    barrier = pltpu.get_barrier_semaphore()
    neighbours = (
        (row, origin(1)),
        (row, origin(-1)),
        (at(lax.rem(x + 1, NX), y, core), z),
        (at(lax.rem(x + NX - 1, NX), y, core), z),
        (at(x, lax.rem(y + 1, NY), core), z),
        (at(x, lax.rem(y + NY - 1, NY), core), z),
        (sibling, z),
    )

    def load_rows(b):
        part = pl.ds(b * block, block)
        return pltpu.make_async_copy(t_hbm.at[part], acc.at[part], tload.at[b])

    def own_panel(p):
        return pltpu.make_async_copy(panels[p], pg.at[p, z], local.at[p])

    inverses = ((inv1_hbm, inv1), (inv2_hbm, inv2))

    def load_inverse(p):
        return pltpu.make_async_copy(*inverses[p], local.at[4 + p])

    for p in range(2):
        own_panel(p).start()
    for n in neighbours:
        pl.semaphore_signal(barrier, inc=1, device_id=n, device_id_type=MESH)
    pl.semaphore_wait(barrier, len(neighbours))

    def where(j):
        return j // nblocks, pl.ds((j % nblocks) * block, block)

    def hops(side, j):
        return half if (j % 2 == side) else half - 1

    def zsend(side, h, j):
        if h > hops(side, j):
            return
        p, lanes = where(j)
        sign = -1 if side == 0 else 1
        owner = origin(sign * (h - 1))
        src = panels[p].at[:, lanes] if h == 1 else pg.at[p, owner, :, lanes]
        dst = last.at[p, :, lanes] if h == half else pg.at[p, owner, :, lanes]
        pltpu.make_async_remote_copy(
            src_ref=src,
            dst_ref=dst,
            send_sem=zs.at[side, h - 1],
            recv_sem=zr.at[side, h - 1, j],
            device_id=(row, origin(-sign)),
            device_id_type=MESH,
        ).start()

    def zwait(side, h, j):
        if h > hops(side, j):
            return
        p, lanes = where(j)
        owner = origin(-h if side == 0 else h)
        ref = last.at[p, :, lanes] if h == half else pg.at[p, owner, :, lanes]
        pltpu.make_async_remote_copy(
            src_ref=ref,
            dst_ref=ref,
            send_sem=zs.at[side, h - 1],
            recv_sem=zr.at[side, h - 1, j],
            device_id=(row, origin(1)),
            device_id_type=MESH,
        ).wait_recv()

    def first(j):
        for side in SIDES:
            zsend(side, 1, j)

    def forward(h, j):
        for side in SIDES:
            zwait(side, h, j)
            zsend(side, h + 1, j)

    buffers = (t1, t2, pb)
    order = [0]
    for d in range(1, half):
        order += [-d, d]
    order += [half]

    def piece(array, i):
        index = i if array < 2 else origin(order[i])
        return pl.ds(pl.multiple_of(index * xp, xp), xp)

    def xcopy(array, i, slot, src, target):
        return pltpu.make_async_remote_copy(
            src_ref=src,
            dst_ref=buffers[array].at[piece(array, i)],
            send_sem=xs.at[array, i % 2, slot],
            recv_sem=xr.at[array, i],
            device_id=(target, z),
            device_id_type=MESH,
        )

    def edges(tree):
        u, v = x, y

        def to(uu, vv):
            return at(uu, vv, core)

        return (
            (jnp.logical_and(v == 0, u <= 1), to(lax.rem(u + 1, NX), v)),
            (jnp.logical_and(v == 0, u == 0), to(NX - 1, v)),
            (v <= 1, to(u, lax.rem(v + 1, NX))),
            (v == 0, to(u, NX - 1)),
        )

    def to_children(array, i, src):
        for slot, (sends, target) in enumerate(edges(i % 2)):
            @pl.when(sends)
            def _():
                xcopy(array, i, slot, src, target).start()

        xcopy(array, i, 4, src, sibling).start()

    def xwait(array, i):
        ref = buffers[array].at[piece(array, i)]
        xcopy(array, i, 4, ref, sibling).wait_recv()

    def xforward(array, i):
        xwait(array, i)

        @pl.when(core == min(array, 1))
        def _():
            to_children(array, i, buffers[array].at[piece(array, i)])

    def drain(array):
        pieces = buffers[array].at[pl.ds(0, block // 2)]

        def wait(tree, slot):
            pltpu.make_async_remote_copy(
                src_ref=pieces, dst_ref=pieces, send_sem=xs.at[array, tree, slot], recv_sem=xr.at[array, 0],
                device_id=(sibling, z), device_id_type=MESH,
            ).wait_send()

        @pl.when(core == min(array, 1))
        def _():
            for tree in range(2):
                for slot, (sends, _unused) in enumerate(edges(tree)):
                    @pl.when(sends)
                    def _():
                        wait(tree, slot)

                wait(tree, 4)

    def keep_rows(array):
        return pltpu.make_async_copy(t_hbm.at[pl.ds(0, block)], buffers[array], local.at[2])

    def held_piece(i):
        lanes = pl.ds(0, block)
        if order[i] == half:
            return last.at[0, :, lanes]
        return pg.at[0, origin(order[i]), :, lanes]

    def keep_panel(i):
        return pltpu.make_async_copy(held_piece(i), pb.at[piece(2, i)], local.at[3])

    def panel_piece(i):
        src = held_piece(i)

        @pl.when(core == 1)
        def _():
            to_children(2, i, src)
            keep_panel(i).start()

    def start_loads():
        for p in range(2):
            load_inverse(p).start()
        for b in range(nblocks):
            load_rows(b).start()

    @pl.when(source)
    def _():
        for array in range(2):
            @pl.when(core == array)
            def _():
                keep_rows(array).start()
                for i in range(nz):
                    to_children(array, i, t_hbm.at[pl.ds(i * xp, xp)])

        first(0)
        first(1)
        start_loads()
        own_panel(0).wait()
        panel_piece(0)
        for h in range(1, half):
            forward(h, 0)
            first(h + 1)
            panel_piece(2 * h - 1)
            panel_piece(2 * h)
        for j in range(half + 1, npieces):
            first(j)
        zwait(0, half, 0)
        panel_piece(nz - 1)
        for array in range(2):
            @pl.when(core == array)
            def _():
                keep_rows(array).wait()

            @pl.when(core != array)
            def _():
                for i in range(nz):
                    xwait(array, i)
        for j in range(1, npieces):
            forward(1, j)

    @pl.when(other)
    def _():
        for j in range(npieces):
            first(j)
        start_loads()
        own_panel(0).wait()
        for i in range(nz):
            xforward(0, i)
            xforward(1, i)
            if i < npieces:
                forward(1, i)

    own_panel(1).wait()

    def keep_split(p, value):
        high, low = split(value)
        sh[p] = high
        sl[p] = low

    rh[...], rl[...] = split(t1[...])
    load_inverse(0).wait()
    s1[...] = product(inv1[...], rh[...], rl[...])
    keep_split(0, s1[...])

    @pl.when(source)
    def _():
        for j in range(1, nblocks):
            forward(2, j)

        @pl.when(core == 1)
        def _():
            pltpu.make_async_copy(pb, pb, local.at[3]).wait()

        @pl.when(core == 0)
        def _():
            for i in range(nz):
                xwait(2, i)

    @pl.when(other)
    def _():
        for i in range(nz):
            xforward(2, i)
            if i >= half:
                forward(2, i - half)

    rh[...], rl[...] = split(t2[...] - turned_product(pb[...], sh[0], sl[0]))
    load_inverse(1).wait()
    s2[...] = product(inv2[...], rh[...], rl[...])
    keep_split(1, s2[...])

    def update(b, origins):
        ks = [pl.ds(pl.multiple_of(o * kc, kc), kc) for o in origins]
        rows = pl.ds(b * block, block)
        acc[rows, :] = acc[rows, :] - turned_product(
            jnp.concatenate([pg[p, o, :, rows] for o in origins for p in range(2)], axis=0),
            jnp.concatenate([sh[p, k, :] for k in ks for p in range(2)], axis=0),
            jnp.concatenate([sl[p, k, :] for k in ks for p in range(2)], axis=0),
        )

    near = (z, origin(-1), origin(1))
    far = (origin(-2), origin(2), origin(-3), origin(3))
    for b in range(nblocks):
        forward(2, nblocks + b)
        load_rows(b).wait()
        update(b, near)

    for j in range(npieces):
        if j == 0:
            @pl.when(other)
            def _():
                forward(half - 1, 0)
        else:
            forward(half - 1, j)
        if j >= nblocks:
            b = j - nblocks
            update(b, far)
            if b == 0:
                @pl.when(row == 0)
                def _():
                    acc[pl.ds(0, block), :] = s1[...]

                @pl.when(row == 1)
                def _():
                    acc[pl.ds(0, block), :] = s2[...]

    final = pl.ds(pl.multiple_of(origin(half) * kc, kc), kc)
    for p in range(2):
        right[0, pl.ds(p * kc, kc), :] = sh[p, final, :]
        right[1, pl.ds(p * kc, kc), :] = sl[p, final, :]
    for b in range(nblocks):
        for j in (b, b + nblocks):
            for side in SIDES:
                if j == 0:
                    @pl.when(other)
                    def _():
                        zwait(side, half, 0)
                else:
                    zwait(side, half, j)
        if b < EARLY:
            finish_block(pl.ds(b * block, block), b == 0, acc, acc, last, right)

    for side in SIDES:
        for h in range(1, half + 1):
            ref = pg.at[:, z] if h < half else pg.at[0, z]
            pltpu.make_async_remote_copy(
                src_ref=ref, dst_ref=ref, send_sem=zs.at[side, h - 1], recv_sem=zr.at[side, h - 1, 0],
                device_id=(row, origin(1)), device_id_type=MESH,
            ).wait_send()
    for array in range(3):
        drain(array)


def finish(block, acc, last, right, out_hbm, late, sems):
    stores = []
    rows = acc.shape[0]
    early = EARLY * block
    for i in range(EARLY):
        part = pl.ds(i * block, block)
        stores.append(pltpu.make_async_copy(acc.at[part], out_hbm.at[part], sems.at[i]))
        stores[-1].start()
    step = (rows - early) // CHUNKS
    for i in range(CHUNKS):
        part = pl.ds(early + i * step, step)
        finish_block(part, False, late, acc, last, right)
        stores.append(pltpu.make_async_copy(late.at[part], out_hbm.at[part], sems.at[EARLY + i]))
        stores[-1].start()
    for copy in stores:
        copy.wait()


def per_device(nz, test_kernel, first_panel, second_panel, first_inverse, second_inverse):
    rows, cols = test_kernel.shape
    kc = first_panel.shape[1]
    block = first_inverse.shape[0]
    vmem = pl.BlockSpec(memory_space=pltpu.VMEM)
    hbm = pl.BlockSpec(memory_space=pl.ANY)
    dma = pltpu.SemaphoreType.DMA
    nblocks = rows // block
    operands = (test_kernel, first_panel.T, second_panel.T, first_inverse, second_inverse)
    acc, last, right = pl.pallas_call(
        kernel,
        out_shape=[
            jax.ShapeDtypeStruct((rows, cols), F32),
            jax.ShapeDtypeStruct((2, kc, rows), F32),
            jax.ShapeDtypeStruct((2, 2 * kc, cols), BF16),
        ],
        in_specs=[hbm] * 5,
        out_specs=[vmem, vmem, vmem],
        scratch_shapes=[
            pltpu.VMEM((2, nz, kc, rows), F32),
            pltpu.VMEM((block, block), F32),
            pltpu.VMEM((block, cols), F32),
            pltpu.VMEM((block, cols), F32),
            pltpu.VMEM((block, block), F32),
            pltpu.VMEM((block, block), F32),
            pltpu.VMEM((block, cols), F32),
            pltpu.VMEM((block, cols), F32),
            pltpu.VMEM((2, block, cols), BF16),
            pltpu.VMEM((2, block, cols), BF16),
            pltpu.VMEM((block, cols), BF16),
            pltpu.VMEM((block, cols), BF16),
            dma((2, nz // 2)),
            dma((2, nz // 2, 2 * nblocks)),
            dma((3, 2, 5)),
            dma((3, nz)),
            dma((6,)),
            dma((nblocks,)),
        ],
        compiler_params=pltpu.CompilerParams(
            collective_id=0, has_side_effects=True, vmem_limit_bytes=VMEM_BYTES
        ),
    )(*[pltpu.with_memory_space_constraint(v, pltpu.HBM) for v in operands])
    return pl.pallas_call(
        functools.partial(finish, block),
        out_shape=jax.ShapeDtypeStruct((rows, cols), F32),
        in_specs=[vmem, vmem, vmem],
        out_specs=hbm,
        scratch_shapes=[
            pltpu.VMEM((rows, cols), F32),
            dma((EARLY + CHUNKS,)),
        ],
        compiler_params=pltpu.CompilerParams(vmem_limit_bytes=FINISH_BYTES),
    )(acc, last, right)


def solution(mesh):
    nz = mesh.shape["col"]

    def run(*args):
        return per_device(nz, *args)

    in_specs = (P("row", "col"), P("row", "col"), P("row", "col"), P(), P())
    return jax.shard_map(run, mesh=mesh, in_specs=in_specs, out_specs=P("row", "col"), check_vma=False)
```

```python
import functools

import jax
import jax.numpy as jnp
from jax import lax
from jax.experimental import pallas as pl
from jax.experimental.pallas import tpu as pltpu
from jax.sharding import PartitionSpec as P

MESH = pl.DeviceIdType.MESH
F32 = jnp.float32
BF16 = jnp.bfloat16
NX, NY = 4, 4
SIDES = (0, 1)
VMEM_BYTES = 36 * 1024 * 1024
FINISH_BYTES = 12 * 1024 * 1024
EARLY = 2
CHUNKS = 4


def split(value):
    high = value.astype(BF16)
    return high, (value - high.astype(F32)).astype(BF16)


def dot(left, right):
    return jnp.dot(left, right, preferred_element_type=F32)


def product(left, right_high, right_low):
    high, low = split(left)
    return dot(high, right_high) + (dot(low, right_high) + dot(high, right_low))


def turned_product(left, right_high, right_low):
    high, low = split(left)
    high, low = high.T, low.T
    return dot(
        jnp.concatenate([high, low, high], axis=1),
        jnp.concatenate([right_high, right_high, right_low], axis=0),
    )


def finish_block(part, first, out, acc, last, right):

    def change():
        left = jnp.concatenate([last[p, :, part] for p in range(2)], axis=0)
        out[part, :] = acc[part, :] - turned_product(left, right[0], right[1])

    if first:
        pl.when(lax.axis_index("row") >= 2)(change)
    else:
        change()


def kernel(
    t_hbm, p1_hbm, p2_hbm, inv1_hbm, inv2_hbm, acc, last, right,
    pg, pb, t1, t2, inv1, inv2, s1, s2, sh, sl, rh, rl,
    zs, zr, xs, xr, local, tload, ready,
):
    nz = pg.shape[1]
    kc = pg.shape[2]
    half = nz // 2
    block = t1.shape[0]
    nblocks = acc.shape[0] // block
    npieces = 2 * nblocks
    xp = block // nz
    row = lax.axis_index("row")
    z = lax.axis_index("col")
    core = lax.rem(row, 2)
    y = lax.rem(row // 2, NY)
    x = row // (2 * NY)

    def at(xx, yy, cc):
        return (xx * NY + yy) * 2 + cc

    sibling = at(x, y, 1 - core)
    source = jnp.logical_and(x == 0, y == 0)
    other = jnp.logical_not(source)
    panels = (p1_hbm, p2_hbm)

    def origin(k):
        return lax.rem(z + (k + nz), nz)

    barrier = pltpu.get_barrier_semaphore()

    def before(k, n):
        return jnp.where(k == n - 1, 0, k - 1)

    parent = jnp.where(y == 0, at(before(x, NX), y, core), at(x, before(y, NY), core))
    children = (
        (jnp.logical_and(y == 0, x <= 1), at(lax.rem(x + 1, NX), y, core)),
        (source, at(NX - 1, y, core)),
        (y <= 1, at(x, lax.rem(y + 1, NY), core)),
        (y == 0, at(x, NY - 1, core)),
    )

    def load_rows(b):
        part = pl.ds(b * block, block)
        return pltpu.make_async_copy(t_hbm.at[part], acc.at[part], tload.at[b])

    def own_panel(p):
        return pltpu.make_async_copy(panels[p], pg.at[p, z], local.at[p])

    inverses = ((inv1_hbm, inv1), (inv2_hbm, inv2))

    def load_inverse(p):
        return pltpu.make_async_copy(*inverses[p], local.at[4 + p])

    for p in range(2):
        own_panel(p).start()
    for n in (origin(1), origin(-1)):
        pl.semaphore_signal(barrier, inc=1, device_id=(row, n), device_id_type=MESH)
    for sends, target in children:
        @pl.when(sends)
        def _():
            pl.semaphore_signal(barrier, inc=1, device_id=(target, z), device_id_type=MESH)

    @pl.when(core == 0)
    def _():
        pl.semaphore_signal(barrier, inc=1, device_id=(sibling, z), device_id_type=MESH)

    pl.semaphore_wait(barrier, 2 + jnp.where(other, 1, 0) + core)

    @pl.when(other)
    def _():
        pl.semaphore_signal(ready, inc=1, device_id=(parent, z), device_id_type=MESH)

    @pl.when(core == 1)
    def _():
        pl.semaphore_signal(ready, inc=1, device_id=(sibling, z), device_id_type=MESH)

    def wait_receivers():
        count = 1 - core
        for sends, _unused in children:
            count = count + jnp.where(sends, 1, 0)

        @pl.when(count > 0)
        def _():
            pl.semaphore_wait(ready, count)

    def where(j):
        return j // nblocks, pl.ds((j % nblocks) * block, block)

    def hops(side, j):
        return half if (j % 2 == side) else half - 1

    def zsend(side, h, j):
        if h > hops(side, j):
            return
        p, lanes = where(j)
        sign = -1 if side == 0 else 1
        owner = origin(sign * (h - 1))
        src = panels[p].at[:, lanes] if h == 1 else pg.at[p, owner, :, lanes]
        dst = last.at[p, :, lanes] if h == half else pg.at[p, owner, :, lanes]
        pltpu.make_async_remote_copy(
            src_ref=src,
            dst_ref=dst,
            send_sem=zs.at[side, h - 1],
            recv_sem=zr.at[side, h - 1, j],
            device_id=(row, origin(-sign)),
            device_id_type=MESH,
        ).start()

    def zwait(side, h, j):
        if h > hops(side, j):
            return
        p, lanes = where(j)
        owner = origin(-h if side == 0 else h)
        ref = last.at[p, :, lanes] if h == half else pg.at[p, owner, :, lanes]
        pltpu.make_async_remote_copy(
            src_ref=ref,
            dst_ref=ref,
            send_sem=zs.at[side, h - 1],
            recv_sem=zr.at[side, h - 1, j],
            device_id=(row, origin(1)),
            device_id_type=MESH,
        ).wait_recv()

    def first(j):
        for side in SIDES:
            zsend(side, 1, j)

    def forward(h, j):
        for side in SIDES:
            zwait(side, h, j)
            zsend(side, h + 1, j)

    buffers = (t1, t2, pb)
    order = [0]
    for d in range(1, half):
        order += [-d, d]
    order += [half]

    def piece(array, i):
        index = i if array < 2 else origin(order[i])
        return pl.ds(pl.multiple_of(index * xp, xp), xp)

    def xcopy(array, i, slot, src, target):
        return pltpu.make_async_remote_copy(
            src_ref=src,
            dst_ref=buffers[array].at[piece(array, i)],
            send_sem=xs.at[array, slot],
            recv_sem=xr.at[array, i],
            device_id=(target, z),
            device_id_type=MESH,
        )

    def to_children(array, i, src):
        for slot, (sends, target) in enumerate(children):
            @pl.when(sends)
            def _():
                xcopy(array, i, slot, src, target).start()

        xcopy(array, i, 4, src, sibling).start()

    def xwait(array, i):
        ref = buffers[array].at[piece(array, i)]
        xcopy(array, i, 4, ref, sibling).wait_recv()

    def xforward(array, i):
        xwait(array, i)

        @pl.when(core == min(array, 1))
        def _():
            to_children(array, i, buffers[array].at[piece(array, i)])

    def drain(array):
        whole = buffers[array]

        def wait(slot):
            pltpu.make_async_remote_copy(
                src_ref=whole, dst_ref=whole, send_sem=xs.at[array, slot], recv_sem=xr.at[array, 0],
                device_id=(sibling, z), device_id_type=MESH,
            ).wait_send()

        @pl.when(core == min(array, 1))
        def _():
            for slot, (sends, _unused) in enumerate(children):
                @pl.when(sends)
                def _():
                    wait(slot)

            wait(len(children))

    def keep_rows(array):
        return pltpu.make_async_copy(t_hbm.at[pl.ds(0, block)], buffers[array], local.at[2])

    def held_piece(i):
        lanes = pl.ds(0, block)
        if order[i] == half:
            return last.at[0, :, lanes]
        return pg.at[0, origin(order[i]), :, lanes]

    def keep_panel(i):
        return pltpu.make_async_copy(held_piece(i), pb.at[piece(2, i)], local.at[3])

    def panel_piece(i):
        src = held_piece(i)

        @pl.when(core == 1)
        def _():
            to_children(2, i, src)
            keep_panel(i).start()

    def start_loads():
        for p in range(2):
            load_inverse(p).start()
        for b in range(nblocks):
            load_rows(b).start()

    @pl.when(source)
    def _():
        for array in range(2):
            @pl.when(core == array)
            def _():
                keep_rows(array).start()

        first(0)
        first(1)
        wait_receivers()
        for array in range(2):
            @pl.when(core == array)
            def _():
                for i in range(nz):
                    to_children(array, i, t_hbm.at[pl.ds(i * xp, xp)])

        start_loads()
        own_panel(0).wait()
        panel_piece(0)
        for h in range(1, half):
            forward(h, 0)
            first(h + 1)
            panel_piece(2 * h - 1)
            panel_piece(2 * h)
        for j in range(half + 1, npieces):
            first(j)
        zwait(0, half, 0)
        panel_piece(nz - 1)
        for array in range(2):
            @pl.when(core == array)
            def _():
                keep_rows(array).wait()

            @pl.when(core != array)
            def _():
                for i in range(nz):
                    xwait(array, i)
        for j in range(1, npieces):
            forward(1, j)

    @pl.when(other)
    def _():
        for j in range(npieces):
            first(j)
        start_loads()
        wait_receivers()
        own_panel(0).wait()
        for i in range(nz):
            xforward(0, i)
            xforward(1, i)
            if i < npieces:
                forward(1, i)

    own_panel(1).wait()

    def keep_split(p, value):
        high, low = split(value)
        sh[p] = high
        sl[p] = low

    rh[...], rl[...] = split(t1[...])
    load_inverse(0).wait()
    s1[...] = product(inv1[...], rh[...], rl[...])
    keep_split(0, s1[...])

    @pl.when(source)
    def _():
        for j in range(1, npieces):
            forward(2, j)

        @pl.when(core == 1)
        def _():
            pltpu.make_async_copy(pb, pb, local.at[3]).wait()

        @pl.when(core == 0)
        def _():
            for i in range(nz):
                xwait(2, i)

    @pl.when(other)
    def _():
        for i in range(nz):
            forward(2, i)
            xforward(2, i)

    rh[...], rl[...] = split(t2[...] - turned_product(pb[...], sh[0], sl[0]))
    load_inverse(1).wait()
    s2[...] = product(inv2[...], rh[...], rl[...])
    keep_split(1, s2[...])

    def update(b, origins):
        ks = [pl.ds(pl.multiple_of(o * kc, kc), kc) for o in origins]
        rows = pl.ds(b * block, block)
        acc[rows, :] = acc[rows, :] - turned_product(
            jnp.concatenate([pg[p, o, :, rows] for o in origins for p in range(2)], axis=0),
            jnp.concatenate([sh[p, k, :] for k in ks for p in range(2)], axis=0),
            jnp.concatenate([sl[p, k, :] for k in ks for p in range(2)], axis=0),
        )

    near = (z, origin(-1), origin(1))
    far = (origin(-2), origin(2), origin(-3), origin(3))
    for b in range(nblocks):
        load_rows(b).wait()
        update(b, near)

    for j in range(npieces):
        if j == 0:
            @pl.when(other)
            def _():
                forward(half - 1, 0)
        else:
            forward(half - 1, j)
        if j >= nblocks:
            b = j - nblocks
            update(b, far)
            if b == 0:
                @pl.when(row == 0)
                def _():
                    acc[pl.ds(0, block), :] = s1[...]

                @pl.when(row == 1)
                def _():
                    acc[pl.ds(0, block), :] = s2[...]

    final = pl.ds(pl.multiple_of(origin(half) * kc, kc), kc)
    for p in range(2):
        right[0, pl.ds(p * kc, kc), :] = sh[p, final, :]
        right[1, pl.ds(p * kc, kc), :] = sl[p, final, :]
    for b in range(nblocks):
        for j in (b, b + nblocks):
            for side in SIDES:
                if j == 0:
                    @pl.when(other)
                    def _():
                        zwait(side, half, 0)
                else:
                    zwait(side, half, j)
        if b < EARLY:
            finish_block(pl.ds(b * block, block), b == 0, acc, acc, last, right)

    for side in SIDES:
        for h in range(1, half + 1):
            ref = pg.at[:, z] if h < half else pg.at[0, z]
            pltpu.make_async_remote_copy(
                src_ref=ref, dst_ref=ref, send_sem=zs.at[side, h - 1], recv_sem=zr.at[side, h - 1, 0],
                device_id=(row, origin(1)), device_id_type=MESH,
            ).wait_send()
    for array in range(3):
        drain(array)


def finish(block, acc, last, right, out_hbm, late, sems):
    stores = []
    rows = acc.shape[0]
    early = EARLY * block
    for i in range(EARLY):
        part = pl.ds(i * block, block)
        stores.append(pltpu.make_async_copy(acc.at[part], out_hbm.at[part], sems.at[i]))
        stores[-1].start()
    step = (rows - early) // CHUNKS
    for i in range(CHUNKS):
        part = pl.ds(early + i * step, step)
        finish_block(part, False, late, acc, last, right)
        stores.append(pltpu.make_async_copy(late.at[part], out_hbm.at[part], sems.at[EARLY + i]))
        stores[-1].start()
    for copy in stores:
        copy.wait()


def per_device(nz, test_kernel, first_panel, second_panel, first_inverse, second_inverse):
    rows, cols = test_kernel.shape
    kc = first_panel.shape[1]
    block = first_inverse.shape[0]
    vmem = pl.BlockSpec(memory_space=pltpu.VMEM)
    hbm = pl.BlockSpec(memory_space=pl.ANY)
    dma = pltpu.SemaphoreType.DMA
    nblocks = rows // block
    operands = (test_kernel, first_panel.T, second_panel.T, first_inverse, second_inverse)
    acc, last, right = pl.pallas_call(
        kernel,
        out_shape=[
            jax.ShapeDtypeStruct((rows, cols), F32),
            jax.ShapeDtypeStruct((2, kc, rows), F32),
            jax.ShapeDtypeStruct((2, 2 * kc, cols), BF16),
        ],
        in_specs=[hbm] * 5,
        out_specs=[vmem, vmem, vmem],
        scratch_shapes=[
            pltpu.VMEM((2, nz, kc, rows), F32),
            pltpu.VMEM((block, block), F32),
            pltpu.VMEM((block, cols), F32),
            pltpu.VMEM((block, cols), F32),
            pltpu.VMEM((block, block), F32),
            pltpu.VMEM((block, block), F32),
            pltpu.VMEM((block, cols), F32),
            pltpu.VMEM((block, cols), F32),
            pltpu.VMEM((2, block, cols), BF16),
            pltpu.VMEM((2, block, cols), BF16),
            pltpu.VMEM((block, cols), BF16),
            pltpu.VMEM((block, cols), BF16),
            dma((2, nz // 2)),
            dma((2, nz // 2, 2 * nblocks)),
            dma((3, 5)),
            dma((3, nz)),
            dma((6,)),
            dma((nblocks,)),
            pltpu.SemaphoreType.REGULAR,
        ],
        compiler_params=pltpu.CompilerParams(
            collective_id=0, has_side_effects=True, vmem_limit_bytes=VMEM_BYTES
        ),
    )(*[pltpu.with_memory_space_constraint(v, pltpu.HBM) for v in operands])
    return pl.pallas_call(
        functools.partial(finish, block),
        out_shape=jax.ShapeDtypeStruct((rows, cols), F32),
        in_specs=[vmem, vmem, vmem],
        out_specs=hbm,
        scratch_shapes=[
            pltpu.VMEM((rows, cols), F32),
            dma((EARLY + CHUNKS,)),
        ],
        compiler_params=pltpu.CompilerParams(vmem_limit_bytes=FINISH_BYTES),
    )(acc, last, right)


def solution(mesh):
    nz = mesh.shape["col"]

    def run(*args):
        return per_device(nz, *args)

    in_specs = (P("row", "col"), P("row", "col"), P("row", "col"), P(), P())
    return jax.shard_map(run, mesh=mesh, in_specs=in_specs, out_specs=P("row", "col"), check_vma=False)
```

```python
import functools

import jax
import jax.numpy as jnp
from jax import lax
from jax.experimental import pallas as pl
from jax.experimental.pallas import tpu as pltpu
from jax.sharding import PartitionSpec as P

MESH = pl.DeviceIdType.MESH
F32 = jnp.float32
BF16 = jnp.bfloat16
NX, NY = 4, 4
SIDES = (0, 1)
VMEM_BYTES = 36 * 1024 * 1024
FINISH_BYTES = 12 * 1024 * 1024
EARLY = 2
CHUNKS = 4


def split(value):
    high = value.astype(BF16)
    return high, (value - high.astype(F32)).astype(BF16)


def dot(left, right):
    return jnp.dot(left, right, preferred_element_type=F32)


def product(left, right_high, right_low):
    high, low = split(left)
    return dot(high, right_high) + (dot(low, right_high) + dot(high, right_low))


def turned_product(left, right_high, right_low):
    high, low = split(left)
    high, low = high.T, low.T
    return dot(
        jnp.concatenate([high, low, high], axis=1),
        jnp.concatenate([right_high, right_high, right_low], axis=0),
    )


def finish_block(part, first, out, acc, last, right):

    def change():
        left = jnp.concatenate([last[p, :, part] for p in range(2)], axis=0)
        out[part, :] = acc[part, :] - turned_product(left, right[0], right[1])

    if first:
        pl.when(lax.axis_index("row") >= 2)(change)
    else:
        change()


def kernel(
    t_hbm, p1_hbm, p2_hbm, inv1_hbm, inv2_hbm, acc, last, right,
    pg, pb, t1, t2, inv1, inv2, s1, s2, sh, sl, rh, rl,
    zs, zr, xs, xr, local, tload, ready, below,
):
    nz = pg.shape[1]
    kc = pg.shape[2]
    half = nz // 2
    block = t1.shape[0]
    nblocks = acc.shape[0] // block
    npieces = 2 * nblocks
    xp = block // nz
    row = lax.axis_index("row")
    z = lax.axis_index("col")
    core = lax.rem(row, 2)
    y = lax.rem(row // 2, NY)
    x = row // (2 * NY)

    def at(xx, yy, cc):
        return (xx * NY + yy) * 2 + cc

    sibling = at(x, y, 1 - core)
    source = jnp.logical_and(x == 0, y == 0)
    other = jnp.logical_not(source)
    panels = (p1_hbm, p2_hbm)

    def origin(k):
        return lax.rem(z + (k + nz), nz)

    barrier = pltpu.get_barrier_semaphore()

    def before(k, n):
        return jnp.where(k == n - 1, 0, k - 1)

    parent = jnp.where(y == 0, at(before(x, NX), y, core), at(x, before(y, NY), core))
    children = (
        (jnp.logical_and(y == 0, x <= 1), at(lax.rem(x + 1, NX), y, core)),
        (source, at(NX - 1, y, core)),
        (y <= 1, at(x, lax.rem(y + 1, NY), core)),
        (y == 0, at(x, NY - 1, core)),
    )

    def load_rows(b):
        part = pl.ds(b * block, block)
        return pltpu.make_async_copy(t_hbm.at[part], acc.at[part], tload.at[b])

    def own_panel(p):
        return pltpu.make_async_copy(panels[p], pg.at[p, z], local.at[p])

    inverses = ((inv1_hbm, inv1), (inv2_hbm, inv2))

    def load_inverse(p):
        return pltpu.make_async_copy(*inverses[p], local.at[4 + p])

    for p in range(2):
        own_panel(p).start()
    pl.semaphore_signal(barrier, inc=1, device_id=(row, origin(-1)), device_id_type=MESH)
    for sends, target in children:
        @pl.when(sends)
        def _():
            pl.semaphore_signal(barrier, inc=1, device_id=(target, z), device_id_type=MESH)

    @pl.when(core == 0)
    def _():
        pl.semaphore_signal(barrier, inc=1, device_id=(sibling, z), device_id_type=MESH)

    pl.semaphore_wait(barrier, 1 + jnp.where(other, 1, 0) + core)
    pl.semaphore_signal(below, inc=1, device_id=(row, origin(1)), device_id_type=MESH)

    @pl.when(other)
    def _():
        pl.semaphore_signal(ready, inc=1, device_id=(parent, z), device_id_type=MESH)

    @pl.when(core == 1)
    def _():
        pl.semaphore_signal(ready, inc=1, device_id=(sibling, z), device_id_type=MESH)

    def wait_receivers():
        count = 1 - core
        for sends, _unused in children:
            count = count + jnp.where(sends, 1, 0)

        @pl.when(count > 0)
        def _():
            pl.semaphore_wait(ready, count)

    def where(j):
        return j // nblocks, pl.ds((j % nblocks) * block, block)

    def hops(side, j):
        return half if (j % 2 == side) else half - 1

    def zsend(side, h, j):
        if h > hops(side, j):
            return
        p, lanes = where(j)
        sign = -1 if side == 0 else 1
        owner = origin(sign * (h - 1))
        src = panels[p].at[:, lanes] if h == 1 else pg.at[p, owner, :, lanes]
        dst = last.at[p, :, lanes] if h == half else pg.at[p, owner, :, lanes]
        pltpu.make_async_remote_copy(
            src_ref=src,
            dst_ref=dst,
            send_sem=zs.at[side, h - 1],
            recv_sem=zr.at[side, h - 1, j],
            device_id=(row, origin(-sign)),
            device_id_type=MESH,
        ).start()

    def zwait(side, h, j):
        if h > hops(side, j):
            return
        p, lanes = where(j)
        owner = origin(-h if side == 0 else h)
        ref = last.at[p, :, lanes] if h == half else pg.at[p, owner, :, lanes]
        pltpu.make_async_remote_copy(
            src_ref=ref,
            dst_ref=ref,
            send_sem=zs.at[side, h - 1],
            recv_sem=zr.at[side, h - 1, j],
            device_id=(row, origin(1)),
            device_id_type=MESH,
        ).wait_recv()

    def first(j):
        for side in SIDES:
            zsend(side, 1, j)

    def start(count):
        for j in range(count):
            zsend(0, 1, j)
        pl.semaphore_wait(below, 1)
        for j in range(count):
            zsend(1, 1, j)

    def forward(h, j):
        for side in SIDES:
            zwait(side, h, j)
            zsend(side, h + 1, j)

    buffers = (t1, t2, pb)
    order = [0]
    for d in range(1, half):
        order += [-d, d]
    order += [half]

    def piece(array, i):
        index = i if array < 2 else origin(order[i])
        return pl.ds(pl.multiple_of(index * xp, xp), xp)

    def xcopy(array, i, slot, src, target):
        return pltpu.make_async_remote_copy(
            src_ref=src,
            dst_ref=buffers[array].at[piece(array, i)],
            send_sem=xs.at[array, slot],
            recv_sem=xr.at[array, i],
            device_id=(target, z),
            device_id_type=MESH,
        )

    def to_children(array, i, src):
        for slot, (sends, target) in enumerate(children):
            @pl.when(sends)
            def _():
                xcopy(array, i, slot, src, target).start()

        xcopy(array, i, 4, src, sibling).start()

    def xwait(array, i):
        ref = buffers[array].at[piece(array, i)]
        xcopy(array, i, 4, ref, sibling).wait_recv()

    def xforward(array, i):
        xwait(array, i)

        @pl.when(core == min(array, 1))
        def _():
            to_children(array, i, buffers[array].at[piece(array, i)])

    def drain(array):
        whole = buffers[array]

        def wait(slot):
            pltpu.make_async_remote_copy(
                src_ref=whole, dst_ref=whole, send_sem=xs.at[array, slot], recv_sem=xr.at[array, 0],
                device_id=(sibling, z), device_id_type=MESH,
            ).wait_send()

        @pl.when(core == min(array, 1))
        def _():
            for slot, (sends, _unused) in enumerate(children):
                @pl.when(sends)
                def _():
                    wait(slot)

            wait(len(children))

    def keep_rows(array):
        return pltpu.make_async_copy(t_hbm.at[pl.ds(0, block)], buffers[array], local.at[2])

    def held_piece(i):
        lanes = pl.ds(0, block)
        if order[i] == half:
            return last.at[0, :, lanes]
        return pg.at[0, origin(order[i]), :, lanes]

    def keep_panel(i):
        return pltpu.make_async_copy(held_piece(i), pb.at[piece(2, i)], local.at[3])

    def panel_piece(i):
        src = held_piece(i)

        @pl.when(core == 1)
        def _():
            to_children(2, i, src)
            keep_panel(i).start()

    def start_loads():
        for p in range(2):
            load_inverse(p).start()
        for b in range(nblocks):
            load_rows(b).start()

    @pl.when(source)
    def _():
        for array in range(2):
            @pl.when(core == array)
            def _():
                keep_rows(array).start()

        start(2)
        wait_receivers()
        for array in range(2):
            @pl.when(core == array)
            def _():
                for i in range(nz):
                    to_children(array, i, t_hbm.at[pl.ds(i * xp, xp)])

        start_loads()
        own_panel(0).wait()
        panel_piece(0)
        for h in range(1, half):
            forward(h, 0)
            first(h + 1)
            panel_piece(2 * h - 1)
            panel_piece(2 * h)
        for j in range(half + 1, npieces):
            first(j)
        zwait(0, half, 0)
        panel_piece(nz - 1)
        for array in range(2):
            @pl.when(core == array)
            def _():
                keep_rows(array).wait()

            @pl.when(core != array)
            def _():
                for i in range(nz):
                    xwait(array, i)
        for j in range(1, npieces):
            forward(1, j)

    @pl.when(other)
    def _():
        start(npieces)
        start_loads()
        wait_receivers()
        own_panel(0).wait()
        for i in range(nz):
            xforward(0, i)
            xforward(1, i)
            if i < npieces:
                forward(1, i)

    own_panel(1).wait()

    def keep_split(p, value):
        high, low = split(value)
        sh[p] = high
        sl[p] = low

    rh[...], rl[...] = split(t1[...])
    load_inverse(0).wait()
    s1[...] = product(inv1[...], rh[...], rl[...])
    keep_split(0, s1[...])

    @pl.when(source)
    def _():
        for j in range(1, npieces):
            forward(2, j)

        @pl.when(core == 1)
        def _():
            pltpu.make_async_copy(pb, pb, local.at[3]).wait()

        @pl.when(core == 0)
        def _():
            for i in range(nz):
                xwait(2, i)

    @pl.when(other)
    def _():
        for i in range(nz):
            forward(2, i)
            xforward(2, i)

    rh[...], rl[...] = split(t2[...] - turned_product(pb[...], sh[0], sl[0]))
    load_inverse(1).wait()
    s2[...] = product(inv2[...], rh[...], rl[...])
    keep_split(1, s2[...])

    def update(b, origins):
        ks = [pl.ds(pl.multiple_of(o * kc, kc), kc) for o in origins]
        rows = pl.ds(b * block, block)
        acc[rows, :] = acc[rows, :] - turned_product(
            jnp.concatenate([pg[p, o, :, rows] for o in origins for p in range(2)], axis=0),
            jnp.concatenate([sh[p, k, :] for k in ks for p in range(2)], axis=0),
            jnp.concatenate([sl[p, k, :] for k in ks for p in range(2)], axis=0),
        )

    near = (z, origin(-1), origin(1))
    far = (origin(-2), origin(2), origin(-3), origin(3))
    for b in range(nblocks):
        load_rows(b).wait()
        update(b, near)

    for j in range(npieces):
        if j == 0:
            @pl.when(other)
            def _():
                forward(half - 1, 0)
        else:
            forward(half - 1, j)
        if j >= nblocks:
            b = j - nblocks
            update(b, far)
            if b == 0:
                @pl.when(row == 0)
                def _():
                    acc[pl.ds(0, block), :] = s1[...]

                @pl.when(row == 1)
                def _():
                    acc[pl.ds(0, block), :] = s2[...]

    final = pl.ds(pl.multiple_of(origin(half) * kc, kc), kc)
    for p in range(2):
        right[0, pl.ds(p * kc, kc), :] = sh[p, final, :]
        right[1, pl.ds(p * kc, kc), :] = sl[p, final, :]
    for b in range(nblocks):
        for j in (b, b + nblocks):
            for side in SIDES:
                if j == 0:
                    @pl.when(other)
                    def _():
                        zwait(side, half, 0)
                else:
                    zwait(side, half, j)
        if b < EARLY:
            finish_block(pl.ds(b * block, block), b == 0, acc, acc, last, right)

    for side in SIDES:
        for h in range(1, half + 1):
            ref = pg.at[:, z] if h < half else pg.at[0, z]
            pltpu.make_async_remote_copy(
                src_ref=ref, dst_ref=ref, send_sem=zs.at[side, h - 1], recv_sem=zr.at[side, h - 1, 0],
                device_id=(row, origin(1)), device_id_type=MESH,
            ).wait_send()
    for array in range(3):
        drain(array)


def finish(block, acc, last, right, out_hbm, late, sems):
    stores = []
    rows = acc.shape[0]
    early = EARLY * block
    for i in range(EARLY):
        part = pl.ds(i * block, block)
        stores.append(pltpu.make_async_copy(acc.at[part], out_hbm.at[part], sems.at[i]))
        stores[-1].start()
    step = (rows - early) // CHUNKS
    for i in range(CHUNKS):
        part = pl.ds(early + i * step, step)
        finish_block(part, False, late, acc, last, right)
        stores.append(pltpu.make_async_copy(late.at[part], out_hbm.at[part], sems.at[EARLY + i]))
        stores[-1].start()
    for copy in stores:
        copy.wait()


def per_device(nz, test_kernel, first_panel, second_panel, first_inverse, second_inverse):
    rows, cols = test_kernel.shape
    kc = first_panel.shape[1]
    block = first_inverse.shape[0]
    vmem = pl.BlockSpec(memory_space=pltpu.VMEM)
    hbm = pl.BlockSpec(memory_space=pl.ANY)
    dma = pltpu.SemaphoreType.DMA
    nblocks = rows // block
    operands = (test_kernel, first_panel.T, second_panel.T, first_inverse, second_inverse)
    acc, last, right = pl.pallas_call(
        kernel,
        out_shape=[
            jax.ShapeDtypeStruct((rows, cols), F32),
            jax.ShapeDtypeStruct((2, kc, rows), F32),
            jax.ShapeDtypeStruct((2, 2 * kc, cols), BF16),
        ],
        in_specs=[hbm] * 5,
        out_specs=[vmem, vmem, vmem],
        scratch_shapes=[
            pltpu.VMEM((2, nz, kc, rows), F32),
            pltpu.VMEM((block, block), F32),
            pltpu.VMEM((block, cols), F32),
            pltpu.VMEM((block, cols), F32),
            pltpu.VMEM((block, block), F32),
            pltpu.VMEM((block, block), F32),
            pltpu.VMEM((block, cols), F32),
            pltpu.VMEM((block, cols), F32),
            pltpu.VMEM((2, block, cols), BF16),
            pltpu.VMEM((2, block, cols), BF16),
            pltpu.VMEM((block, cols), BF16),
            pltpu.VMEM((block, cols), BF16),
            dma((2, nz // 2)),
            dma((2, nz // 2, 2 * nblocks)),
            dma((3, 5)),
            dma((3, nz)),
            dma((6,)),
            dma((nblocks,)),
            pltpu.SemaphoreType.REGULAR,
            pltpu.SemaphoreType.REGULAR,
        ],
        compiler_params=pltpu.CompilerParams(
            collective_id=0, has_side_effects=True, vmem_limit_bytes=VMEM_BYTES
        ),
    )(*[pltpu.with_memory_space_constraint(v, pltpu.HBM) for v in operands])
    return pl.pallas_call(
        functools.partial(finish, block),
        out_shape=jax.ShapeDtypeStruct((rows, cols), F32),
        in_specs=[vmem, vmem, vmem],
        out_specs=hbm,
        scratch_shapes=[
            pltpu.VMEM((rows, cols), F32),
            dma((EARLY + CHUNKS,)),
        ],
        compiler_params=pltpu.CompilerParams(vmem_limit_bytes=FINISH_BYTES),
    )(acc, last, right)


def solution(mesh):
    nz = mesh.shape["col"]

    def run(*args):
        return per_device(nz, *args)

    in_specs = (P("row", "col"), P("row", "col"), P("row", "col"), P(), P())
    return jax.shard_map(run, mesh=mesh, in_specs=in_specs, out_specs=P("row", "col"), check_vma=False)
```

```python
import functools

import jax
import jax.numpy as jnp
from jax import lax
from jax.experimental import pallas as pl
from jax.experimental.pallas import tpu as pltpu
from jax.sharding import PartitionSpec as P

MESH = pl.DeviceIdType.MESH
F32 = jnp.float32
BF16 = jnp.bfloat16
NX, NY = 4, 4
SIDES = (0, 1)
VMEM_BYTES = 36 * 1024 * 1024
FINISH_BYTES = 12 * 1024 * 1024
EARLY = 2
CHUNKS = 4


def split(value):
    high = value.astype(BF16)
    return high, (value - high.astype(F32)).astype(BF16)


def dot(left, right):
    return jnp.dot(left, right, preferred_element_type=F32)


def product(left, right_high, right_low):
    high, low = split(left)
    return dot(high, right_high) + (dot(low, right_high) + dot(high, right_low))


def turned_product(left, right_high, right_low):
    high, low = split(left)
    high, low = high.T, low.T
    return dot(
        jnp.concatenate([high, low, high], axis=1),
        jnp.concatenate([right_high, right_high, right_low], axis=0),
    )


def finish_block(part, first, out, acc, last, right):

    def change():
        left = jnp.concatenate([last[p, :, part] for p in range(2)], axis=0)
        out[part, :] = acc[part, :] - turned_product(left, right[0], right[1])

    if first:
        pl.when(lax.axis_index("row") >= 2)(change)
    else:
        change()


def kernel(
    t_hbm, p1_hbm, p2_hbm, inv1_hbm, inv2_hbm, acc, last, right,
    pg, pb, t1, t2, inv1, inv2, s1, s2, sh, sl, rh, rl,
    zs, zr, xs, xr, local, tload, ready, below,
):
    nz = pg.shape[1]
    kc = pg.shape[2]
    half = nz // 2
    block = t1.shape[0]
    nblocks = acc.shape[0] // block
    npieces = nblocks + nblocks // 2
    xp = block // nz
    row = lax.axis_index("row")
    z = lax.axis_index("col")
    core = lax.rem(row, 2)
    y = lax.rem(row // 2, NY)
    x = row // (2 * NY)

    def at(xx, yy, cc):
        return (xx * NY + yy) * 2 + cc

    sibling = at(x, y, 1 - core)
    source = jnp.logical_and(x == 0, y == 0)
    other = jnp.logical_not(source)
    panels = (p1_hbm, p2_hbm)

    def origin(k):
        return lax.rem(z + (k + nz), nz)

    barrier = pltpu.get_barrier_semaphore()

    def before(k, n):
        return jnp.where(k == n - 1, 0, k - 1)

    parent = jnp.where(y == 0, at(before(x, NX), y, core), at(x, before(y, NY), core))
    children = (
        (jnp.logical_and(y == 0, x <= 1), at(lax.rem(x + 1, NX), y, core)),
        (source, at(NX - 1, y, core)),
        (y <= 1, at(x, lax.rem(y + 1, NY), core)),
        (y == 0, at(x, NY - 1, core)),
    )

    def load_rows(b):
        part = pl.ds(b * block, block)
        return pltpu.make_async_copy(t_hbm.at[part], acc.at[part], tload.at[b])

    def own_panel(p):
        return pltpu.make_async_copy(panels[p], pg.at[p, z], local.at[p])

    inverses = ((inv1_hbm, inv1), (inv2_hbm, inv2))

    def load_inverse(p):
        return pltpu.make_async_copy(*inverses[p], local.at[4 + p])

    pl.semaphore_signal(barrier, inc=1, device_id=(row, origin(-1)), device_id_type=MESH)
    for sends, target in children:
        @pl.when(sends)
        def _():
            pl.semaphore_signal(barrier, inc=1, device_id=(target, z), device_id_type=MESH)

    @pl.when(core == 0)
    def _():
        pl.semaphore_signal(barrier, inc=1, device_id=(sibling, z), device_id_type=MESH)

    pl.semaphore_wait(barrier, 1 + jnp.where(other, 1, 0) + core)
    pl.semaphore_signal(below, inc=1, device_id=(row, origin(1)), device_id_type=MESH)

    def answer():
        @pl.when(other)
        def _():
            pl.semaphore_signal(ready, inc=1, device_id=(parent, z), device_id_type=MESH)

        @pl.when(core == 1)
        def _():
            pl.semaphore_signal(ready, inc=1, device_id=(sibling, z), device_id_type=MESH)

    def wait_receivers():
        count = 1 - core
        for sends, _unused in children:
            count = count + jnp.where(sends, 1, 0)

        @pl.when(count > 0)
        def _():
            pl.semaphore_wait(ready, count)

    def where(j):
        if j < nblocks:
            return 0, pl.ds(j * block, block)
        return 1, pl.ds((j - nblocks) * 2 * block, 2 * block)

    def second(b):
        return nblocks + b // 2

    def hops(side, j):
        return half if (j % 2 == side) else half - 1

    def zsend(side, h, j):
        if h > hops(side, j):
            return
        p, lanes = where(j)
        sign = -1 if side == 0 else 1
        owner = origin(sign * (h - 1))
        src = panels[p].at[:, lanes] if h == 1 else pg.at[p, owner, :, lanes]
        dst = last.at[p, :, lanes] if h == half else pg.at[p, owner, :, lanes]
        pltpu.make_async_remote_copy(
            src_ref=src,
            dst_ref=dst,
            send_sem=zs.at[side, h - 1],
            recv_sem=zr.at[side, h - 1, j],
            device_id=(row, origin(-sign)),
            device_id_type=MESH,
        ).start()

    def zwait(side, h, j):
        if h > hops(side, j):
            return
        p, lanes = where(j)
        owner = origin(-h if side == 0 else h)
        ref = last.at[p, :, lanes] if h == half else pg.at[p, owner, :, lanes]
        pltpu.make_async_remote_copy(
            src_ref=ref,
            dst_ref=ref,
            send_sem=zs.at[side, h - 1],
            recv_sem=zr.at[side, h - 1, j],
            device_id=(row, origin(1)),
            device_id_type=MESH,
        ).wait_recv()

    def first(j):
        for side in SIDES:
            zsend(side, 1, j)

    def start(count):
        for j in range(count):
            zsend(0, 1, j)
        answer()
        for p in range(2):
            own_panel(p).start()
        pl.semaphore_wait(below, 1)
        for j in range(count):
            zsend(1, 1, j)

    def forward(h, j):
        for side in SIDES:
            zwait(side, h, j)
            zsend(side, h + 1, j)

    buffers = (t1, t2, pb)
    order = [0]
    for d in range(1, half):
        order += [-d, d]
    order += [half]

    def piece(array, i):
        index = i if array < 2 else origin(order[i])
        return pl.ds(pl.multiple_of(index * xp, xp), xp)

    def xcopy(array, i, slot, src, target):
        return pltpu.make_async_remote_copy(
            src_ref=src,
            dst_ref=buffers[array].at[piece(array, i)],
            send_sem=xs.at[array, slot],
            recv_sem=xr.at[array, i],
            device_id=(target, z),
            device_id_type=MESH,
        )

    def to_children(array, i, src):
        for slot, (sends, target) in enumerate(children):
            @pl.when(sends)
            def _():
                xcopy(array, i, slot, src, target).start()

        xcopy(array, i, 4, src, sibling).start()

    def xwait(array, i):
        ref = buffers[array].at[piece(array, i)]
        xcopy(array, i, 4, ref, sibling).wait_recv()

    def xforward(array, i):
        xwait(array, i)

        @pl.when(core == min(array, 1))
        def _():
            to_children(array, i, buffers[array].at[piece(array, i)])

    def drain(array):
        whole = buffers[array]

        def wait(slot):
            pltpu.make_async_remote_copy(
                src_ref=whole, dst_ref=whole, send_sem=xs.at[array, slot], recv_sem=xr.at[array, 0],
                device_id=(sibling, z), device_id_type=MESH,
            ).wait_send()

        @pl.when(core == min(array, 1))
        def _():
            for slot, (sends, _unused) in enumerate(children):
                @pl.when(sends)
                def _():
                    wait(slot)

            wait(len(children))

    def keep_rows(array):
        return pltpu.make_async_copy(t_hbm.at[pl.ds(0, block)], buffers[array], local.at[2])

    def held_piece(i):
        lanes = pl.ds(0, block)
        if order[i] == half:
            return last.at[0, :, lanes]
        return pg.at[0, origin(order[i]), :, lanes]

    def keep_panel(i):
        return pltpu.make_async_copy(held_piece(i), pb.at[piece(2, i)], local.at[3])

    def panel_piece(i):
        src = held_piece(i)

        @pl.when(core == 1)
        def _():
            to_children(2, i, src)
            keep_panel(i).start()

    def start_loads():
        for p in range(2):
            load_inverse(p).start()
        for b in range(nblocks):
            load_rows(b).start()

    @pl.when(source)
    def _():
        for array in range(2):
            @pl.when(core == array)
            def _():
                keep_rows(array).start()

        start(2)
        wait_receivers()
        for array in range(2):
            @pl.when(core == array)
            def _():
                for i in range(nz):
                    to_children(array, i, t_hbm.at[pl.ds(i * xp, xp)])

        start_loads()
        own_panel(0).wait()
        panel_piece(0)
        for h in range(1, half):
            forward(h, 0)
            first(h + 1)
            panel_piece(2 * h - 1)
            panel_piece(2 * h)
        for j in range(half + 1, npieces):
            first(j)
        zwait(0, half, 0)
        panel_piece(nz - 1)
        for array in range(2):
            @pl.when(core == array)
            def _():
                keep_rows(array).wait()

            @pl.when(core != array)
            def _():
                for i in range(nz):
                    xwait(array, i)
        for j in range(1, npieces):
            forward(1, j)

    @pl.when(other)
    def _():
        start(npieces)
        start_loads()
        wait_receivers()
        own_panel(0).wait()
        for i in range(nz):
            xforward(0, i)
            xforward(1, i)
            if i < npieces:
                forward(1, i)

    own_panel(1).wait()

    def keep_split(p, value):
        high, low = split(value)
        sh[p] = high
        sl[p] = low

    rh[...], rl[...] = split(t1[...])
    load_inverse(0).wait()
    s1[...] = product(inv1[...], rh[...], rl[...])
    keep_split(0, s1[...])

    @pl.when(source)
    def _():
        for j in range(1, npieces):
            forward(2, j)

        @pl.when(core == 1)
        def _():
            pltpu.make_async_copy(pb, pb, local.at[3]).wait()

        @pl.when(core == 0)
        def _():
            for i in range(nz):
                xwait(2, i)

    @pl.when(other)
    def _():
        for i in range(nz):
            if i < npieces:
                forward(2, i)
            xforward(2, i)

    rh[...], rl[...] = split(t2[...] - turned_product(pb[...], sh[0], sl[0]))
    load_inverse(1).wait()
    s2[...] = product(inv2[...], rh[...], rl[...])
    keep_split(1, s2[...])

    def update(b, origins):
        ks = [pl.ds(pl.multiple_of(o * kc, kc), kc) for o in origins]
        rows = pl.ds(b * block, block)
        acc[rows, :] = acc[rows, :] - turned_product(
            jnp.concatenate([pg[p, o, :, rows] for o in origins for p in range(2)], axis=0),
            jnp.concatenate([sh[p, k, :] for k in ks for p in range(2)], axis=0),
            jnp.concatenate([sl[p, k, :] for k in ks for p in range(2)], axis=0),
        )

    near = (z, origin(-1), origin(1))
    far = (origin(-2), origin(2), origin(-3), origin(3))
    for b in range(nblocks):
        load_rows(b).wait()
        update(b, near)

    for pair in range(nblocks // 2):
        b = 2 * pair
        for k in (b, b + 1, second(b)) if b < EARLY else (b + 1, b, second(b)):
            if k == 0:
                @pl.when(other)
                def _():
                    forward(half - 1, 0)
            else:
                forward(half - 1, k)
        for b in (2 * pair, 2 * pair + 1):
            update(b, far)
            if b == 0:
                @pl.when(row == 0)
                def _():
                    acc[pl.ds(0, block), :] = s1[...]

                @pl.when(row == 1)
                def _():
                    acc[pl.ds(0, block), :] = s2[...]

    final = pl.ds(pl.multiple_of(origin(half) * kc, kc), kc)
    for p in range(2):
        right[0, pl.ds(p * kc, kc), :] = sh[p, final, :]
        right[1, pl.ds(p * kc, kc), :] = sl[p, final, :]
    for b in range(nblocks):
        for j in (b, second(b)) if b % 2 == 0 else (b,):
            for side in SIDES:
                if j == 0:
                    @pl.when(other)
                    def _():
                        zwait(side, half, 0)
                else:
                    zwait(side, half, j)
        if b < EARLY:
            finish_block(pl.ds(b * block, block), b == 0, acc, acc, last, right)

    for side in SIDES:
        for h in range(1, half + 1):
            ref = pg.at[:, z] if h < half else pg.at[0, z]
            pltpu.make_async_remote_copy(
                src_ref=ref, dst_ref=ref, send_sem=zs.at[side, h - 1], recv_sem=zr.at[side, h - 1, 0],
                device_id=(row, origin(1)), device_id_type=MESH,
            ).wait_send()
    for array in range(3):
        drain(array)


def finish(block, acc, last, right, out_hbm, late, sems):
    stores = []
    rows = acc.shape[0]
    early = EARLY * block
    for i in range(EARLY):
        part = pl.ds(i * block, block)
        stores.append(pltpu.make_async_copy(acc.at[part], out_hbm.at[part], sems.at[i]))
        stores[-1].start()
    step = (rows - early) // CHUNKS
    for i in range(CHUNKS):
        part = pl.ds(early + i * step, step)
        finish_block(part, False, late, acc, last, right)
        stores.append(pltpu.make_async_copy(late.at[part], out_hbm.at[part], sems.at[EARLY + i]))
        stores[-1].start()
    for copy in stores:
        copy.wait()


def per_device(nz, test_kernel, first_panel, second_panel, first_inverse, second_inverse):
    rows, cols = test_kernel.shape
    kc = first_panel.shape[1]
    block = first_inverse.shape[0]
    vmem = pl.BlockSpec(memory_space=pltpu.VMEM)
    hbm = pl.BlockSpec(memory_space=pl.ANY)
    dma = pltpu.SemaphoreType.DMA
    nblocks = rows // block
    operands = (test_kernel, first_panel.T, second_panel.T, first_inverse, second_inverse)
    acc, last, right = pl.pallas_call(
        kernel,
        out_shape=[
            jax.ShapeDtypeStruct((rows, cols), F32),
            jax.ShapeDtypeStruct((2, kc, rows), F32),
            jax.ShapeDtypeStruct((2, 2 * kc, cols), BF16),
        ],
        in_specs=[hbm] * 5,
        out_specs=[vmem, vmem, vmem],
        scratch_shapes=[
            pltpu.VMEM((2, nz, kc, rows), F32),
            pltpu.VMEM((block, block), F32),
            pltpu.VMEM((block, cols), F32),
            pltpu.VMEM((block, cols), F32),
            pltpu.VMEM((block, block), F32),
            pltpu.VMEM((block, block), F32),
            pltpu.VMEM((block, cols), F32),
            pltpu.VMEM((block, cols), F32),
            pltpu.VMEM((2, block, cols), BF16),
            pltpu.VMEM((2, block, cols), BF16),
            pltpu.VMEM((block, cols), BF16),
            pltpu.VMEM((block, cols), BF16),
            dma((2, nz // 2)),
            dma((2, nz // 2, 2 * nblocks)),
            dma((3, 5)),
            dma((3, nz)),
            dma((6,)),
            dma((nblocks,)),
            pltpu.SemaphoreType.REGULAR,
            pltpu.SemaphoreType.REGULAR,
        ],
        compiler_params=pltpu.CompilerParams(
            collective_id=0, has_side_effects=True, vmem_limit_bytes=VMEM_BYTES
        ),
    )(*[pltpu.with_memory_space_constraint(v, pltpu.HBM) for v in operands])
    return pl.pallas_call(
        functools.partial(finish, block),
        out_shape=jax.ShapeDtypeStruct((rows, cols), F32),
        in_specs=[vmem, vmem, vmem],
        out_specs=hbm,
        scratch_shapes=[
            pltpu.VMEM((rows, cols), F32),
            dma((EARLY + CHUNKS,)),
        ],
        compiler_params=pltpu.CompilerParams(vmem_limit_bytes=FINISH_BYTES),
    )(acc, last, right)


def solution(mesh):
    nz = mesh.shape["col"]

    def run(*args):
        return per_device(nz, *args)

    in_specs = (P("row", "col"), P("row", "col"), P("row", "col"), P(), P())
    return jax.shard_map(run, mesh=mesh, in_specs=in_specs, out_specs=P("row", "col"), check_vma=False)
```

```python
import functools

import jax
import jax.numpy as jnp
from jax import lax
from jax.experimental import pallas as pl
from jax.experimental.pallas import tpu as pltpu
from jax.sharding import PartitionSpec as P

MESH = pl.DeviceIdType.MESH
F32 = jnp.float32
BF16 = jnp.bfloat16
NX, NY = 4, 4
SIDES = (0, 1)
VMEM_BYTES = 36 * 1024 * 1024
FINISH_BYTES = 12 * 1024 * 1024
EARLY = 2
CHUNKS = 2


def split(value):
    high = value.astype(BF16)
    return high, (value - high.astype(F32)).astype(BF16)


def dot(left, right):
    return jnp.dot(left, right, preferred_element_type=F32)


def product(left, right_high, right_low):
    high, low = split(left)
    return dot(high, right_high) + (dot(low, right_high) + dot(high, right_low))


def turned_product(left, right_high, right_low):
    high, low = split(left)
    high, low = high.T, low.T
    return dot(
        jnp.concatenate([high, low, high], axis=1),
        jnp.concatenate([right_high, right_high, right_low], axis=0),
    )


def finish_block(part, first, out, acc, last, right):

    def change():
        left = jnp.concatenate([last[p, :, part] for p in range(2)], axis=0)
        out[part, :] = acc[part, :] - turned_product(left, right[0], right[1])

    if first:
        pl.when(lax.axis_index("row") >= 2)(change)
    else:
        change()


def kernel(
    t_hbm, p1_hbm, p2_hbm, inv1_hbm, inv2_hbm, acc, last, right,
    pg, pb, t1, t2, inv1, inv2, s1, s2, sh, sl, rh, rl,
    zs, zr, xs, xr, local, tload, ready, below,
):
    nz = pg.shape[1]
    kc = pg.shape[2]
    half = nz // 2
    block = t1.shape[0]
    nblocks = acc.shape[0] // block
    npieces = nblocks + nblocks // 2
    xp = block // nz
    row = lax.axis_index("row")
    z = lax.axis_index("col")
    core = lax.rem(row, 2)
    y = lax.rem(row // 2, NY)
    x = row // (2 * NY)

    def at(xx, yy, cc):
        return (xx * NY + yy) * 2 + cc

    sibling = at(x, y, 1 - core)
    source = jnp.logical_and(x == 0, y == 0)
    other = jnp.logical_not(source)
    panels = (p1_hbm, p2_hbm)

    def origin(k):
        return lax.rem(z + (k + nz), nz)

    barrier = pltpu.get_barrier_semaphore()

    def before(k, n):
        return jnp.where(k == n - 1, 0, k - 1)

    parent = jnp.where(y == 0, at(before(x, NX), y, core), at(x, before(y, NY), core))
    children = (
        (jnp.logical_and(y == 0, x <= 1), at(lax.rem(x + 1, NX), y, core)),
        (source, at(NX - 1, y, core)),
        (y <= 1, at(x, lax.rem(y + 1, NY), core)),
        (y == 0, at(x, NY - 1, core)),
    )

    def load_rows(b):
        part = pl.ds(b * block, block)
        return pltpu.make_async_copy(t_hbm.at[part], acc.at[part], tload.at[b])

    def own_panel(p):
        return pltpu.make_async_copy(panels[p], pg.at[p, z], local.at[p])

    inverses = ((inv1_hbm, inv1), (inv2_hbm, inv2))

    def load_inverse(p):
        return pltpu.make_async_copy(*inverses[p], local.at[4 + p])

    pl.semaphore_signal(barrier, inc=1, device_id=(row, origin(-1)), device_id_type=MESH)
    for sends, target in children:
        @pl.when(sends)
        def _():
            pl.semaphore_signal(barrier, inc=1, device_id=(target, z), device_id_type=MESH)

    @pl.when(core == 0)
    def _():
        pl.semaphore_signal(barrier, inc=1, device_id=(sibling, z), device_id_type=MESH)

    pl.semaphore_wait(barrier, 1 + jnp.where(other, 1, 0) + core)
    pl.semaphore_signal(below, inc=1, device_id=(row, origin(1)), device_id_type=MESH)

    def answer():
        @pl.when(other)
        def _():
            pl.semaphore_signal(ready, inc=1, device_id=(parent, z), device_id_type=MESH)

        @pl.when(core == 1)
        def _():
            pl.semaphore_signal(ready, inc=1, device_id=(sibling, z), device_id_type=MESH)

    def wait_receivers():
        count = 1 - core
        for sends, _unused in children:
            count = count + jnp.where(sends, 1, 0)

        @pl.when(count > 0)
        def _():
            pl.semaphore_wait(ready, count)

    def where(j):
        if j < nblocks:
            return 0, pl.ds(j * block, block)
        return 1, pl.ds((j - nblocks) * 2 * block, 2 * block)

    def second(b):
        return nblocks + b // 2

    def hops(side, j):
        return half if (j % 2 == side) else half - 1

    def zsend(side, h, j):
        if h > hops(side, j):
            return
        p, lanes = where(j)
        sign = -1 if side == 0 else 1
        owner = origin(sign * (h - 1))
        src = panels[p].at[:, lanes] if h == 1 else pg.at[p, owner, :, lanes]
        dst = last.at[p, :, lanes] if h == half else pg.at[p, owner, :, lanes]
        pltpu.make_async_remote_copy(
            src_ref=src,
            dst_ref=dst,
            send_sem=zs.at[side, h - 1],
            recv_sem=zr.at[side, h - 1, j],
            device_id=(row, origin(-sign)),
            device_id_type=MESH,
        ).start()

    def zwait(side, h, j):
        if h > hops(side, j):
            return
        p, lanes = where(j)
        owner = origin(-h if side == 0 else h)
        ref = last.at[p, :, lanes] if h == half else pg.at[p, owner, :, lanes]
        pltpu.make_async_remote_copy(
            src_ref=ref,
            dst_ref=ref,
            send_sem=zs.at[side, h - 1],
            recv_sem=zr.at[side, h - 1, j],
            device_id=(row, origin(1)),
            device_id_type=MESH,
        ).wait_recv()

    def first(j):
        for side in SIDES:
            zsend(side, 1, j)

    def start(count):
        for j in range(count):
            zsend(0, 1, j)
        answer()
        for p in range(2):
            own_panel(p).start()
        pl.semaphore_wait(below, 1)
        for j in range(count):
            zsend(1, 1, j)

    def forward(h, j):
        for side in SIDES:
            zwait(side, h, j)
            zsend(side, h + 1, j)

    buffers = (t1, t2, pb)
    order = [0]
    for d in range(1, half):
        order += [-d, d]
    order += [half]

    def piece(array, i):
        index = i if array < 2 else origin(order[i])
        return pl.ds(pl.multiple_of(index * xp, xp), xp)

    def xcopy(array, i, slot, src, target):
        return pltpu.make_async_remote_copy(
            src_ref=src,
            dst_ref=buffers[array].at[piece(array, i)],
            send_sem=xs.at[array, slot],
            recv_sem=xr.at[array, i],
            device_id=(target, z),
            device_id_type=MESH,
        )

    def to_children(array, i, src):
        for slot, (sends, target) in enumerate(children):
            @pl.when(sends)
            def _():
                xcopy(array, i, slot, src, target).start()

        xcopy(array, i, 4, src, sibling).start()

    def xwait(array, i):
        ref = buffers[array].at[piece(array, i)]
        xcopy(array, i, 4, ref, sibling).wait_recv()

    def xforward(array, i):
        xwait(array, i)

        @pl.when(core == min(array, 1))
        def _():
            to_children(array, i, buffers[array].at[piece(array, i)])

    def drain(array):
        whole = buffers[array]

        def wait(slot):
            pltpu.make_async_remote_copy(
                src_ref=whole, dst_ref=whole, send_sem=xs.at[array, slot], recv_sem=xr.at[array, 0],
                device_id=(sibling, z), device_id_type=MESH,
            ).wait_send()

        @pl.when(core == min(array, 1))
        def _():
            for slot, (sends, _unused) in enumerate(children):
                @pl.when(sends)
                def _():
                    wait(slot)

            wait(len(children))

    def keep_rows(array):
        return pltpu.make_async_copy(t_hbm.at[pl.ds(0, block)], buffers[array], local.at[2])

    def held_piece(i):
        lanes = pl.ds(0, block)
        if order[i] == half:
            return last.at[0, :, lanes]
        return pg.at[0, origin(order[i]), :, lanes]

    def keep_panel(i):
        return pltpu.make_async_copy(held_piece(i), pb.at[piece(2, i)], local.at[3])

    def panel_piece(i):
        src = held_piece(i)

        @pl.when(core == 1)
        def _():
            to_children(2, i, src)
            keep_panel(i).start()

    def start_loads():
        for p in range(2):
            load_inverse(p).start()
        for b in range(nblocks):
            load_rows(b).start()

    @pl.when(source)
    def _():
        for array in range(2):
            @pl.when(core == array)
            def _():
                keep_rows(array).start()

        start(2)
        wait_receivers()
        for array in range(2):
            @pl.when(core == array)
            def _():
                for i in range(nz):
                    to_children(array, i, t_hbm.at[pl.ds(i * xp, xp)])

        start_loads()
        own_panel(0).wait()
        panel_piece(0)
        for h in range(1, half):
            forward(h, 0)
            first(h + 1)
            panel_piece(2 * h - 1)
            panel_piece(2 * h)
        for j in range(half + 1, npieces):
            first(j)
        zwait(0, half, 0)
        panel_piece(nz - 1)
        for array in range(2):
            @pl.when(core == array)
            def _():
                keep_rows(array).wait()

            @pl.when(core != array)
            def _():
                for i in range(nz):
                    xwait(array, i)
        for j in range(1, npieces):
            forward(1, j)

    @pl.when(other)
    def _():
        start(npieces)
        start_loads()
        wait_receivers()
        own_panel(0).wait()
        for i in range(nz):
            xforward(0, i)
            xforward(1, i)
            if i < npieces:
                forward(1, i)

    own_panel(1).wait()

    def keep_split(p, value):
        high, low = split(value)
        sh[p] = high
        sl[p] = low

    rh[...], rl[...] = split(t1[...])
    load_inverse(0).wait()
    s1[...] = product(inv1[...], rh[...], rl[...])
    keep_split(0, s1[...])

    @pl.when(source)
    def _():
        for j in range(1, npieces):
            forward(2, j)

        @pl.when(core == 1)
        def _():
            pltpu.make_async_copy(pb, pb, local.at[3]).wait()

        @pl.when(core == 0)
        def _():
            for i in range(nz):
                xwait(2, i)

    @pl.when(other)
    def _():
        for i in range(nz):
            if i < npieces:
                forward(2, i)
            xforward(2, i)

    rh[...], rl[...] = split(t2[...] - turned_product(pb[...], sh[0], sl[0]))
    load_inverse(1).wait()
    s2[...] = product(inv2[...], rh[...], rl[...])
    keep_split(1, s2[...])

    def update(b, origins):
        ks = [pl.ds(pl.multiple_of(o * kc, kc), kc) for o in origins]
        rows = pl.ds(b * block, block)
        acc[rows, :] = acc[rows, :] - turned_product(
            jnp.concatenate([pg[p, o, :, rows] for o in origins for p in range(2)], axis=0),
            jnp.concatenate([sh[p, k, :] for k in ks for p in range(2)], axis=0),
            jnp.concatenate([sl[p, k, :] for k in ks for p in range(2)], axis=0),
        )

    near = (z, origin(-1), origin(1))
    far = (origin(-2), origin(2), origin(-3), origin(3))
    for b in range(nblocks):
        load_rows(b).wait()
        update(b, near)

    for pair in range(nblocks // 2):
        b = 2 * pair
        for k in (b, b + 1, second(b)) if b < EARLY else (b + 1, b, second(b)):
            if k == 0:
                @pl.when(other)
                def _():
                    forward(half - 1, 0)
            else:
                forward(half - 1, k)
        for b in (2 * pair, 2 * pair + 1):
            update(b, far)
            if b == 0:
                @pl.when(row == 0)
                def _():
                    acc[pl.ds(0, block), :] = s1[...]

                @pl.when(row == 1)
                def _():
                    acc[pl.ds(0, block), :] = s2[...]

    final = pl.ds(pl.multiple_of(origin(half) * kc, kc), kc)
    for p in range(2):
        right[0, pl.ds(p * kc, kc), :] = sh[p, final, :]
        right[1, pl.ds(p * kc, kc), :] = sl[p, final, :]
    for b in range(nblocks):
        for j in (b, second(b)) if b % 2 == 0 else (b,):
            for side in SIDES:
                if j == 0:
                    @pl.when(other)
                    def _():
                        zwait(side, half, 0)
                else:
                    zwait(side, half, j)
        if b < EARLY:
            finish_block(pl.ds(b * block, block), b == 0, acc, acc, last, right)

    for side in SIDES:
        for h in range(1, half + 1):
            ref = pg.at[:, z] if h < half else pg.at[0, z]
            pltpu.make_async_remote_copy(
                src_ref=ref, dst_ref=ref, send_sem=zs.at[side, h - 1], recv_sem=zr.at[side, h - 1, 0],
                device_id=(row, origin(1)), device_id_type=MESH,
            ).wait_send()
    for array in range(3):
        drain(array)


def finish(block, acc, last, right, out_hbm, late, sems):
    stores = []
    rows = acc.shape[0]
    early = EARLY * block
    for i in range(EARLY):
        part = pl.ds(i * block, block)
        stores.append(pltpu.make_async_copy(acc.at[part], out_hbm.at[part], sems.at[i]))
        stores[-1].start()
    step = (rows - early) // CHUNKS
    for i in range(CHUNKS):
        part = pl.ds(early + i * step, step)
        finish_block(part, False, late, acc, last, right)
        stores.append(pltpu.make_async_copy(late.at[part], out_hbm.at[part], sems.at[EARLY + i]))
        stores[-1].start()
    for copy in stores:
        copy.wait()


def per_device(nz, test_kernel, first_panel, second_panel, first_inverse, second_inverse):
    rows, cols = test_kernel.shape
    kc = first_panel.shape[1]
    block = first_inverse.shape[0]
    vmem = pl.BlockSpec(memory_space=pltpu.VMEM)
    hbm = pl.BlockSpec(memory_space=pl.ANY)
    dma = pltpu.SemaphoreType.DMA
    nblocks = rows // block
    operands = (test_kernel, first_panel.T, second_panel.T, first_inverse, second_inverse)
    acc, last, right = pl.pallas_call(
        kernel,
        out_shape=[
            jax.ShapeDtypeStruct((rows, cols), F32),
            jax.ShapeDtypeStruct((2, kc, rows), F32),
            jax.ShapeDtypeStruct((2, 2 * kc, cols), BF16),
        ],
        in_specs=[hbm] * 5,
        out_specs=[vmem, vmem, vmem],
        scratch_shapes=[
            pltpu.VMEM((2, nz, kc, rows), F32),
            pltpu.VMEM((block, block), F32),
            pltpu.VMEM((block, cols), F32),
            pltpu.VMEM((block, cols), F32),
            pltpu.VMEM((block, block), F32),
            pltpu.VMEM((block, block), F32),
            pltpu.VMEM((block, cols), F32),
            pltpu.VMEM((block, cols), F32),
            pltpu.VMEM((2, block, cols), BF16),
            pltpu.VMEM((2, block, cols), BF16),
            pltpu.VMEM((block, cols), BF16),
            pltpu.VMEM((block, cols), BF16),
            dma((2, nz // 2)),
            dma((2, nz // 2, 2 * nblocks)),
            dma((3, 5)),
            dma((3, nz)),
            dma((6,)),
            dma((nblocks,)),
            pltpu.SemaphoreType.REGULAR,
            pltpu.SemaphoreType.REGULAR,
        ],
        compiler_params=pltpu.CompilerParams(
            collective_id=0, has_side_effects=True, vmem_limit_bytes=VMEM_BYTES
        ),
    )(*[pltpu.with_memory_space_constraint(v, pltpu.HBM) for v in operands])
    return pl.pallas_call(
        functools.partial(finish, block),
        out_shape=jax.ShapeDtypeStruct((rows, cols), F32),
        in_specs=[vmem, vmem, vmem],
        out_specs=hbm,
        scratch_shapes=[
            pltpu.VMEM((rows, cols), F32),
            dma((EARLY + CHUNKS,)),
        ],
        compiler_params=pltpu.CompilerParams(vmem_limit_bytes=FINISH_BYTES),
    )(acc, last, right)


def solution(mesh):
    nz = mesh.shape["col"]

    def run(*args):
        return per_device(nz, *args)

    in_specs = (P("row", "col"), P("row", "col"), P("row", "col"), P(), P())
    return jax.shard_map(run, mesh=mesh, in_specs=in_specs, out_specs=P("row", "col"), check_vma=False)
```
